128 devices in a mesh: blk: 16 (over z, x_hi, core), narrow: 8 (over x_lo, y).
Axes of the slice: x: 4 (x_hi: 2, x_lo: 2; x = x_hi * 2 + x_lo), y: 4, z: 4, core: 2. Of those that a mesh axis runs over, the one named last changes fastest.
Arguments:
- student_img: bfloat16 [16384, 1152], P(('blk', 'narrow')), may hold values from -6 to 6
- student_txt: bfloat16 [16384, 1152], P(('blk', 'narrow')), may hold values from -6 to 6
- teacher_img: bfloat16 [16384, 1536], P(('blk', 'narrow')), may hold values from -6 to 6
- teacher_txt: bfloat16 [16384, 1536], P(('blk', 'narrow')), may hold values from -6 to 6
Outputs:
- image_grad: float32 [16384, 1152], P(('blk', 'narrow'))
- text_grad: float32 [16384, 1152], P(('blk', 'narrow'))
The draws below stay inside these ranges and needn't reach their ends.
All inputs are finite; a program needn't handle non-finite values.
Results may differ from the reference program's by a relative error of at most 0.0097.
Values may be sent and summed in bfloat16 or wider, within the bound.
A program may use at most 128 MiB of HBM per device.

```python
import math
import jax
import jax.numpy as jnp
from jax import lax

STUDENT_WIDTH = 1152
TEACHER_WIDTH = 1536
BATCH = 16384


def steps_of(own_key, extent, shards, smallest, top_value):
    def one(axis_at, shards_of):
        steps = jax.random.uniform(jax.random.fold_in(jax.random.fold_in(own_key, 6), axis_at), (shards_of,), jnp.float32, smallest / len(shards), top_value / len(shards))
        return jnp.repeat(jnp.exp(steps), extent[axis_at] // shards_of).reshape((-1,) + (1,) * (len(extent) - axis_at - 1))

    level = one(*shards[0])
    for cut in shards[1:]:
        level = level * one(*cut)
    return level


def noise(rng, extent, spread, limit, cuts=(), kind=jnp.bfloat16):
    array = jax.random.normal(rng, extent, jnp.float32) * spread
    if len(cuts) > 0:
        array = steps_of(rng, extent, cuts, -0.22, 0.18) * array
    return jnp.clip(array, min=-limit, max=limit).astype(kind)


def setup_inputs(seed: int = 0) -> dict:
    arg_keys = jax.random.split(jax.random.key(seed), 5)
    student_img = noise(arg_keys[0], (BATCH, STUDENT_WIDTH), 1.0, 6.0, ((0, 128),))
    student_txt = noise(arg_keys[1], (BATCH, STUDENT_WIDTH), 1.0, 6.0, ((0, 128),))
    teacher_img = noise(arg_keys[2], (BATCH, TEACHER_WIDTH), 1.0, 6.0, ((0, 128),))
    teacher_txt = noise(arg_keys[3], (BATCH, TEACHER_WIDTH), 1.0, 6.0, ((0, 128),))
    return {"student_img": student_img, "student_txt": student_txt, "teacher_img": teacher_img, "teacher_txt": teacher_txt}


epsilon = 1e-06
logit_scale = 100.0
logit_bias = -4.0

def unit_rows(raw_rows):
    raw_float = raw_rows.astype(jnp.float32)
    radius = jnp.sqrt(lax.optimization_barrier(jnp.sum(raw_float * raw_float, axis=1, keepdims=True)) + epsilon)
    return (raw_float / radius, radius)

def unit_back(grad_unit, unit_float, radius):
    along_unit = lax.optimization_barrier(jnp.sum(unit_float * grad_unit, axis=1, keepdims=True))
    return (grad_unit - unit_float * along_unit) / radius

def reference(student_img, student_txt, teacher_img, teacher_txt):
    img_float, img_radius = unit_rows(student_img)
    txt_float, txt_radius = unit_rows(student_txt)
    img_unit = img_float.astype(jnp.bfloat16)
    txt_unit = txt_float.astype(jnp.bfloat16)
    t_img_unit = unit_rows(teacher_img)[0].astype(jnp.bfloat16)
    t_txt_unit = unit_rows(teacher_txt)[0].astype(jnp.bfloat16)
    total_rows = student_img.shape[0]
    embed_width = student_img.shape[1]
    block_rows = math.gcd(total_rows, 512)
    col_ids = jnp.arange(total_rows, dtype=jnp.int32)[None, :]

    def one_block(txt_acc, block_index):
        first_row = (block_index * block_rows).astype(jnp.int32)
        img_block = lax.dynamic_slice_in_dim(img_unit, first_row, block_rows, 0)
        timg_block = lax.dynamic_slice_in_dim(t_img_unit, first_row, block_rows, 0)
        teacher_logit = logit_scale * jnp.dot(timg_block, t_txt_unit.T, preferred_element_type=jnp.float32) + logit_bias
        student_logit = logit_scale * jnp.dot(img_block, txt_unit.T, preferred_element_type=jnp.float32) + logit_bias
        row_ids = first_row + jnp.arange(block_rows, dtype=jnp.int32)[:, None]
        positive = jnp.where(row_ids == col_ids, 1.0, 0.0).astype(jnp.float32)
        pair_grad = (2.0 * jax.nn.sigmoid(student_logit) - jax.nn.sigmoid(teacher_logit) - positive).astype(jnp.bfloat16)
        img_grad = logit_scale * jnp.dot(pair_grad, txt_unit, preferred_element_type=jnp.float32)
        txt_acc = txt_acc + jnp.dot(pair_grad.T, img_block, preferred_element_type=jnp.float32)
        return (txt_acc, img_grad)
    txt_acc, img_blocks = lax.scan(one_block, jnp.zeros((total_rows, embed_width), jnp.float32), jnp.arange(total_rows // block_rows, dtype=jnp.int32))
    img_grad_unit = img_blocks.reshape(total_rows, embed_width)
    image_grad = unit_back(img_grad_unit, img_float, img_radius)
    text_grad = unit_back(logit_scale * txt_acc, txt_float, txt_radius)
    return (image_grad, text_grad)
```

```python
import jax
import jax.numpy as jnp
from jax import lax
from jax.experimental import pallas as pl
from jax.experimental.pallas import tpu as pltpu
from jax.sharding import PartitionSpec as P

epsilon = 1e-06
logit_scale = 100.0
logit_bias = -4.0
half_scale = 0.5 * logit_scale
half_bias = 0.5 * logit_bias

ROWS = 128
MESH_ID = pl.DeviceIdType.MESH
NT = (((1,), (1,)), ((), ()))
NN = (((1,), (0,)), ((), ()))
TN = (((0,), (0,)), ((), ()))


def dot(a, b, dims):
    return lax.dot_general(a, b, dims, preferred_element_type=jnp.float32)


def unit_of(raw):
    x = raw.astype(jnp.float32)
    radius = jnp.sqrt(jnp.sum(x * x, axis=1, keepdims=True) + epsilon)
    return x / radius, radius


def back(grad, raw):
    unit, radius = unit_of(raw)
    along = jnp.sum(unit * grad, axis=1, keepdims=True)
    return (grad - unit * along) / radius


def kernel(
    img_raw, txt_raw, timg_raw, ttxt_raw, image_grad, text_grad,
    si, ti, st, tt, gs, iacc, tacc, ib, tb, ts, crecv, irecv, trecv,
    send_si, send_ti, send_st, send_tt, recv_si, recv_ti, recv_st, recv_tt,
    csend_st, csend_tt, crecv_st, crecv_tt, csend_g, crecv_g, isend, irsem, tsend, trsem,
):
    b = lax.axis_index("blk")
    n = lax.axis_index("narrow")
    core = lax.rem(b, 2)
    z = b // 4
    x = 2 * lax.rem(b // 2, 2) + n // 4
    y = lax.rem(n, 4)
    odd = lax.rem(x, 2)

    def device(x, y, z, core):
        return ((z * 2 + x // 2) * 2 + core, lax.rem(x, 2) * 4 + y)

    def step(v, by):
        return lax.rem(v + 4 + by, 4)

    x_img = x + 1 - 2 * odd
    x_txt = lax.rem(x + 3 + 2 * odd, 4)
    img_up = device(x, step(y, 1), z, core)
    img_down = device(x, step(y, -1), z, core)
    img_far = device(x, step(y, 2), z, core)
    img_side = device(x_img, y, z, core)
    txt_up = device(x, y, step(z, 1), core)
    txt_down = device(x, y, step(z, -1), core)
    txt_far = device(x, y, step(z, 2), core)
    txt_side = device(x_txt, y, z, core)
    twin = device(x, y, z, 1 - core)

    barrier = pltpu.get_barrier_semaphore()
    for peer in (img_up, img_down, img_far, img_side, txt_up, txt_down, txt_far, txt_side, twin):
        pl.semaphore_signal(barrier, inc=1, device_id=peer, device_id_type=MESH_ID)

    ti[0:ROWS] = unit_of(timg_raw[...])[0].astype(jnp.bfloat16)
    tt[0:ROWS] = unit_of(ttxt_raw[...])[0].astype(jnp.bfloat16)
    si[0:ROWS] = unit_of(img_raw[...])[0].astype(jnp.bfloat16)
    st[0:ROWS] = unit_of(txt_raw[...])[0].astype(jnp.bfloat16)

    pl.semaphore_wait(barrier, 9)

    sent = []

    def remote(src, dst, ssem, rsem, dev):
        copy = pltpu.make_async_remote_copy(
            src_ref=src, dst_ref=dst, send_sem=ssem, recv_sem=rsem, device_id=dev, device_id_type=MESH_ID
        )
        copy.start()
        sent.append(copy)
        return copy

    arrays = {
        "ti": (ti, send_ti, recv_ti, ROWS, (img_up, img_down, img_side)),
        "si": (si, send_si, recv_si, ROWS, (img_up, img_down, img_side)),
        "tt": (tt, send_tt, recv_tt, 2 * ROWS, (txt_up, txt_down, txt_side)),
        "st": (st, send_st, recv_st, 2 * ROWS, (txt_up, txt_down, txt_side)),
    }
    got = {}

    def hop(name, src, dst, way):
        ref, ssem, rsem, pitch, devs = arrays[name]
        got[name, dst] = remote(
            ref.at[pl.ds(src * pitch, ROWS)], ref.at[pl.ds(dst * pitch, ROWS)],
            ssem.at[dst], rsem.at[dst], devs[way],
        )

    def across(name, place):
        ref, _, _, pitch, _ = arrays[name]
        ssem, rsem = (csend_tt, crecv_tt) if name == "tt" else (csend_st, crecv_st)
        got[name + "c", place] = remote(
            ref.at[pl.ds(place * pitch, ROWS)], ref.at[pl.ds(place * pitch + ROWS, ROWS)],
            ssem.at[place], rsem.at[place], twin,
        )

    def arrive(*keys):
        for key in keys:
            got[key].wait_recv()

    UP, DOWN, SIDE = 0, 1, 2
    for names in (("ti", "tt"), ("si", "st")):
        for name in names:
            hop(name, 0, 2, UP)
            hop(name, 0, 1, DOWN)
            hop(name, 0, 3, SIDE)
    across("tt", 0)
    across("st", 0)

    def clear(i, _):
        rows = pl.ds(pl.multiple_of(i * ROWS, ROWS), ROWS)
        iacc[rows, :] = jnp.zeros((ROWS, iacc.shape[1]), jnp.float32)
        tacc[pl.ds(pl.multiple_of(i * 2 * ROWS, 2 * ROWS), 2 * ROWS), :] = jnp.zeros(
            (2 * ROWS, tacc.shape[1]), jnp.float32
        )
        return 0

    lax.fori_loop(0, 8, clear, 0)

    arrive(("ti", 1), ("tt", 1))
    for name in ("ti", "tt"):
        hop(name, 1, 4, DOWN)
    arrive(("ti", 3), ("tt", 3), ("ti", 2), ("tt", 2))
    for name in ("ti", "tt"):
        hop(name, 3, 6, UP)
        hop(name, 3, 5, DOWN)
    for place in (1, 2, 3):
        across("tt", place)
    arrive(("si", 2), ("st", 2))
    for name in ("si", "st"):
        hop(name, 2, 4, UP)
    arrive(("si", 3), ("st", 3), ("si", 1), ("st", 1))
    for name in ("si", "st"):
        hop(name, 3, 6, UP)
        hop(name, 3, 5, DOWN)
    for place in (1, 2, 3):
        across("st", place)

    def pair_value(zs, zt):
        return 0.5 + jnp.tanh(half_scale * zs + half_bias) - 0.5 * jnp.tanh(half_scale * zt + half_bias)

    def block(first, count, place, diagonal):
        rows = slice(first, first + count)
        cols = pl.ds(pl.multiple_of(place * 2 * ROWS, 2 * ROWS), 2 * ROWS)
        zt = dot(ti[rows], tt[cols, :], NT)
        zs = dot(si[rows], st[cols, :], NT)
        if diagonal:
            row = lax.broadcasted_iota(jnp.int32, (ROWS, 2 * ROWS), 0)
            col = lax.broadcasted_iota(jnp.int32, (ROWS, 2 * ROWS), 1)
            positive = jnp.where(row == col + place * 4 * ROWS, 1.0, 0.0)
            gs[0:ROWS] = (pair_value(zs[:ROWS], zt[:ROWS]) - positive).astype(jnp.bfloat16)
            gs[ROWS:count] = pair_value(zs[ROWS:], zt[ROWS:]).astype(jnp.bfloat16)
        else:
            gs[0:count] = pair_value(zs, zt).astype(jnp.bfloat16)
        g = gs[0:count]
        iacc[rows] += dot(g, st[cols, :], NN)
        tacc[cols, :] += dot(g, si[rows], TN)

    def blocks(first, count, begin, end, diagonal=False):
        def one(place, _):
            block(first, count, place, diagonal)
            return 0

        lax.fori_loop(begin, end, one, 0)

    arrive(*[(name, place) for place in range(4) for name in ("ttc", "stc")])
    blocks(0, 512, 0, 4, True)

    arrive(("ti", 4), ("tt", 4))
    for name in ("ti", "tt"):
        hop(name, 4, 7, SIDE)
    across("tt", 4)
    arrive(("si", 4), ("st", 4))
    for name in ("si", "st"):
        hop(name, 4, 7, SIDE)
    across("st", 4)
    blocks(512, 128, 0, 4)
    arrive(("ttc", 4), ("stc", 4))
    blocks(0, 640, 4, 5)

    for place in (5, 6, 7):
        arrive(("tt", place))
        across("tt", place)
    for place in (5, 6, 7):
        arrive(("st", place))
        across("st", place)
    arrive(*[(name, place) for place in (5, 6, 7) for name in ("ti", "si")])
    blocks(640, 384, 0, 5)

    def give(places):
        for p in places:
            lo = p * 2 * ROWS + ROWS
            tb[p * ROWS : (p + 1) * ROWS] = tacc[lo : lo + ROWS].astype(jnp.bfloat16)
        for p in places:
            rows = pl.ds(p * ROWS, ROWS)
            got["g", p] = remote(tb.at[rows], crecv.at[rows], csend_g.at[p], crecv_g.at[p], twin)

    give(range(5))
    arrive(*[(name, place) for place in (5, 6, 7) for name in ("ttc", "stc")])
    blocks(0, 1024, 5, 8)
    give((5, 6, 7))

    def own_txt(p):
        return tacc[p * 2 * ROWS : p * 2 * ROWS + ROWS] + crecv[p * ROWS : (p + 1) * ROWS].astype(jnp.float32)

    def at(ref, p):
        return ref.at[pl.ds(p * ROWS, ROWS)]

    def put_img(p, slot, dev):
        got["i", slot] = remote(at(ib, p), at(irecv, slot), isend.at[slot], irsem.at[slot], dev)

    def put_txt(p, slot, dev):
        got["t", slot] = remote(at(ts, p), at(trecv, slot), tsend.at[slot], trsem.at[slot], dev)

    def came(ref, slot):
        return ref[slot * ROWS : (slot + 1) * ROWS].astype(jnp.float32)

    for p in (7, 5, 6, 1, 2):
        ib[p * ROWS : (p + 1) * ROWS] = iacc[p * ROWS : (p + 1) * ROWS].astype(jnp.bfloat16)
    put_img(7, 0, img_side)
    put_img(5, 1, img_up)
    put_img(6, 2, img_down)
    put_img(1, 3, img_up)
    put_img(2, 4, img_down)
    arrive(*[("g", p) for p in range(8)])
    for p in (7, 5, 6, 1, 2):
        ts[p * ROWS : (p + 1) * ROWS] = own_txt(p).astype(jnp.bfloat16)
    put_txt(7, 0, txt_side)
    put_txt(5, 1, txt_up)
    put_txt(6, 2, txt_down)
    put_txt(1, 3, txt_up)
    put_txt(2, 4, txt_down)

    arrive(("i", 0))
    ib[4 * ROWS : 5 * ROWS] = (iacc[4 * ROWS : 5 * ROWS] + came(irecv, 0)).astype(jnp.bfloat16)
    put_img(4, 5, img_far)
    arrive(("i", 1), ("i", 2))
    ib[3 * ROWS : 4 * ROWS] = (iacc[3 * ROWS : 4 * ROWS] + came(irecv, 1) + came(irecv, 2)).astype(jnp.bfloat16)
    put_img(3, 6, img_side)
    arrive(("t", 0))
    ts[4 * ROWS : 5 * ROWS] = (own_txt(4) + came(trecv, 0)).astype(jnp.bfloat16)
    put_txt(4, 5, txt_far)
    arrive(("t", 1), ("t", 2))
    ts[3 * ROWS : 4 * ROWS] = (own_txt(3) + came(trecv, 1) + came(trecv, 2)).astype(jnp.bfloat16)
    put_txt(3, 6, txt_side)

    arrive(*[("i", slot) for slot in (3, 4, 5, 6)])
    total = iacc[0:ROWS] + came(irecv, 3) + came(irecv, 4) + came(irecv, 5) + came(irecv, 6)
    image_grad[...] = back(logit_scale * total, img_raw[...])
    arrive(*[("t", slot) for slot in (3, 4, 5, 6)])
    total = own_txt(0) + came(trecv, 3) + came(trecv, 4) + came(trecv, 5) + came(trecv, 6)
    text_grad[...] = back(logit_scale * total, txt_raw[...])

    for copy in sent:
        copy.wait_send()


def body(student_img, student_txt, teacher_img, teacher_txt):
    width = student_img.shape[1]
    t_width = teacher_img.shape[1]
    bf16, f32 = jnp.bfloat16, jnp.float32
    vmem = pl.BlockSpec(memory_space=pltpu.VMEM)
    dma = pltpu.SemaphoreType.DMA((8,))
    return pl.pallas_call(
        kernel,
        out_shape=[jax.ShapeDtypeStruct((ROWS, width), f32)] * 2,
        in_specs=[vmem] * 4,
        out_specs=[vmem] * 2,
        scratch_shapes=[
            pltpu.VMEM((8 * ROWS, width), bf16),
            pltpu.VMEM((8 * ROWS, t_width), bf16),
            pltpu.VMEM((16 * ROWS, width), bf16),
            pltpu.VMEM((16 * ROWS, t_width), bf16),
            pltpu.VMEM((8 * ROWS, 2 * ROWS), bf16),
            pltpu.VMEM((8 * ROWS, width), f32),
            pltpu.VMEM((16 * ROWS, width), f32),
            pltpu.VMEM((8 * ROWS, width), bf16),
            pltpu.VMEM((8 * ROWS, width), bf16),
            pltpu.VMEM((8 * ROWS, width), bf16),
            pltpu.VMEM((8 * ROWS, width), bf16),
            pltpu.VMEM((7 * ROWS, width), bf16),
            pltpu.VMEM((7 * ROWS, width), bf16),
        ]
        + [dma] * 18,
        compiler_params=pltpu.CompilerParams(
            collective_id=0, has_side_effects=True, vmem_limit_bytes=62 << 20
        ),
    )(student_img, student_txt, teacher_img, teacher_txt)


def solution(mesh):
    rows = P(("blk", "narrow"), None)
    return jax.shard_map(body, mesh=mesh, in_specs=(rows,) * 4, out_specs=(rows, rows), check_vma=False)
```

```python
import jax
import jax.numpy as jnp
from jax import lax
from jax.experimental import pallas as pl
from jax.experimental.pallas import tpu as pltpu
from jax.sharding import PartitionSpec as P

epsilon = 1e-06
logit_scale = 100.0
logit_bias = -4.0
half_scale = 0.5 * logit_scale
half_bias = 0.5 * logit_bias

ROWS = 128
MESH_ID = pl.DeviceIdType.MESH
NT = (((1,), (1,)), ((), ()))
NN = (((1,), (0,)), ((), ()))
TN = (((0,), (0,)), ((), ()))

HALF = ROWS // 2


def dot(a, b, dims):
    return lax.dot_general(a, b, dims, preferred_element_type=jnp.float32)


def unit_of(raw):
    x = raw.astype(jnp.float32)
    radius = jnp.sqrt(jnp.sum(x * x, axis=1, keepdims=True) + epsilon)
    return x / radius, radius


def back(grad, raw):
    unit, radius = unit_of(raw)
    along = jnp.sum(unit * grad, axis=1, keepdims=True)
    return (grad - unit * along) / radius


def kernel(
    img_raw, txt_raw, timg_raw, ttxt_raw, image_grad, text_grad,
    si, ti, st, tt, ps, gs, iacc, tacc, ib, tb, ts, crecv, irecv, trecv,
    send_si, send_ti, send_st, send_tt, recv_si, recv_ti, recv_st, recv_tt,
    csend_st, csend_tt, crecv_st, crecv_tt, csend_g, crecv_g, isend, irsem, tsend, trsem,
):
    b = lax.axis_index("blk")
    n = lax.axis_index("narrow")
    core = lax.rem(b, 2)
    z = b // 4
    x = 2 * lax.rem(b // 2, 2) + n // 4
    y = lax.rem(n, 4)
    odd = lax.rem(x, 2)

    def device(x, y, z, core):
        return ((z * 2 + x // 2) * 2 + core, lax.rem(x, 2) * 4 + y)

    def step(v, by):
        return lax.rem(v + 4 + by, 4)

    x_img = x + 1 - 2 * odd
    x_txt = lax.rem(x + 3 + 2 * odd, 4)
    img_up = device(x, step(y, 1), z, core)
    img_down = device(x, step(y, -1), z, core)
    img_far = device(x, step(y, 2), z, core)
    img_side = device(x_img, y, z, core)
    txt_up = device(x, y, step(z, 1), core)
    txt_down = device(x, y, step(z, -1), core)
    txt_far = device(x, y, step(z, 2), core)
    txt_side = device(x_txt, y, z, core)
    twin = device(x, y, z, 1 - core)

    barrier = pltpu.get_barrier_semaphore()
    for peer in (img_up, img_down, img_far, img_side, txt_up, txt_down, txt_far, txt_side, twin):
        pl.semaphore_signal(barrier, inc=1, device_id=peer, device_id_type=MESH_ID)

    ti[0:ROWS] = unit_of(timg_raw[...])[0].astype(jnp.bfloat16)
    tt[0:ROWS] = unit_of(ttxt_raw[...])[0].astype(jnp.bfloat16)

    pl.semaphore_wait(barrier, 9)

    sent = []

    def remote(src, dst, ssem, rsem, dev):
        copy = pltpu.make_async_remote_copy(
            src_ref=src, dst_ref=dst, send_sem=ssem, recv_sem=rsem, device_id=dev, device_id_type=MESH_ID
        )
        copy.start()
        sent.append(copy)
        return copy

    img_devs = (img_up, img_down, img_side)
    txt_devs = (txt_up, txt_down, txt_side)
    arrays = {
        "ti": (ti, send_ti, recv_ti, ROWS, img_devs),
        "si": (si, send_si, recv_si, ROWS, img_devs),
        "tt": (tt, send_tt, recv_tt, 2 * ROWS, txt_devs),
        "st": (st, send_st, recv_st, 2 * ROWS, txt_devs),
    }
    got = {}
    UP, DOWN, SIDE = 0, 1, 2
    places = {
        "0": (0, 0, ROWS), "1": (1, 0, ROWS), "2": (2, 0, ROWS), "3": (3, 0, ROWS), "4": (4, 0, ROWS),
        "7": (5, 0, ROWS), "1b": (1, HALF, HALF), "2a": (2, 0, HALF), "3a": (3, 0, HALF), "3b": (3, HALF, HALF),
        "4a": (4, 0, HALF), "4b": (4, HALF, HALF),
        "5a": (6, 0, HALF), "6a": (6, HALF, HALF), "5b": (7, 0, HALF), "6b": (7, HALF, HALF),
    }
    index = {"1": 0, "2": 1, "3": 2, "4a": 3, "4b": 4, "7": 5, "5a": 6, "6a": 7, "5b": 8, "6b": 9}

    def hop(name, src, dst, way):
        ref, ssem, rsem, pitch, devs = arrays[name]
        s_slot, s_row, count = places[src]
        d_slot, d_row, _ = places[dst]
        got[name, dst] = remote(
            ref.at[pl.ds(s_slot * pitch + s_row, count)], ref.at[pl.ds(d_slot * pitch + d_row, count)],
            ssem.at[index[dst]], rsem.at[index[dst]], devs[way],
        )

    def across(name, slot):
        ref, _, _, pitch, _ = arrays[name]
        ssem, rsem = (csend_tt, crecv_tt) if name == "tt" else (csend_st, crecv_st)
        got[name + "c", slot] = remote(
            ref.at[pl.ds(slot * pitch, ROWS)], ref.at[pl.ds(slot * pitch + ROWS, ROWS)],
            ssem.at[slot], rsem.at[slot], twin,
        )

    def arrive(*keys):
        for key in keys:
            got[key].wait_recv()

    def first_hops(names):
        for name in names:
            hop(name, "0", "2", UP)
            hop(name, "0", "1", DOWN)
            hop(name, "0", "3", SIDE)

    first_hops(("ti", "tt"))
    across("tt", 0)
    si[0:ROWS] = unit_of(img_raw[...])[0].astype(jnp.bfloat16)
    st[0:ROWS] = unit_of(txt_raw[...])[0].astype(jnp.bfloat16)
    first_hops(("si", "st"))
    across("st", 0)

    def clear(i, _):
        rows = pl.ds(pl.multiple_of(i * ROWS, ROWS), ROWS)
        iacc[rows, :] = jnp.zeros((ROWS, iacc.shape[1]), jnp.float32)
        tacc[pl.ds(pl.multiple_of(i * 2 * ROWS, 2 * ROWS), 2 * ROWS), :] = jnp.zeros(
            (2 * ROWS, tacc.shape[1]), jnp.float32
        )
        return 0

    lax.fori_loop(0, 8, clear, 0)

    def teacher_value(zt):
        return 0.5 - 0.5 * jnp.tanh(half_scale * zt + half_bias)

    def columns(slot):
        return pl.ds(pl.multiple_of(slot * 2 * ROWS, 2 * ROWS), 2 * ROWS)

    def gradients(first, count, slot, teacher, diagonal):
        rows = slice(first, first + count)
        cols = columns(slot)
        zs = dot(si[rows], st[cols, :], NT)
        value = jnp.tanh(half_scale * zs + half_bias) + teacher
        if diagonal:
            row = lax.broadcasted_iota(jnp.int32, (ROWS, 2 * ROWS), 0)
            col = lax.broadcasted_iota(jnp.int32, (ROWS, 2 * ROWS), 1)
            positive = jnp.where(row == col + slot * 4 * ROWS, 1.0, 0.0)
            gs[0:ROWS] = (value[:ROWS] - positive).astype(jnp.bfloat16)
            gs[ROWS:count] = value[ROWS:].astype(jnp.bfloat16)
        else:
            gs[0:count] = value.astype(jnp.bfloat16)
        g = gs[0:count]
        iacc[rows] += dot(g, st[cols, :], NN)
        tacc[cols, :] += dot(g, si[rows], TN)

    def over(begin, end, one):
        lax.fori_loop(begin, end, lambda slot, _: (one(slot), 0)[1], 0)

    def whole(first, count, begin, end, diagonal=False):
        def one(slot):
            zt = dot(ti[first : first + count], tt[columns(slot), :], NT)
            gradients(first, count, slot, teacher_value(zt), diagonal)

        over(begin, end, one)

    def teach(first, count, begin, end):
        def one(slot):
            zt = dot(ti[first : first + count], tt[columns(slot), :], NT)
            ps[slot, first : first + count, :] = teacher_value(zt)

        over(begin, end, one)

    def learn(first, count, begin, end):
        def one(slot):
            gradients(first, count, slot, ps[slot, first : first + count, :], False)

        over(begin, end, one)

    def relay(names):
        for name in names:
            hop(name, "2a", "4a", UP)
            hop(name, "1b", "4b", DOWN)

    def to_ring(names):
        for half in "ab":
            for name in names:
                hop(name, "3" + half, "6" + half, UP)
                hop(name, "3" + half, "5" + half, DOWN)

    def second_hops(names):
        arrive(*[(name, part) for part in ("4a", "4b") for name in names])
        for name in names:
            hop(name, "4", "7", SIDE)
        across(names[1], 4)

    arrive(*[(name, part) for part in "123" for name in ("ti", "tt")])
    relay(("ti", "tt"))
    for slot in (1, 2, 3):
        across("tt", slot)
    arrive(*[(name, part) for part in "123" for name in ("si", "st")])
    relay(("si", "st"))
    to_ring(("ti", "tt"))
    to_ring(("si", "st"))
    for slot in (1, 2, 3):
        across("st", slot)

    arrive(*[(name, slot) for slot in range(4) for name in ("ttc", "stc")])
    whole(0, 512, 0, 2, True)
    second_hops(("ti", "tt"))
    whole(0, 512, 2, 4)
    second_hops(("si", "st"))
    whole(512, 128, 0, 4)
    arrive(("ttc", 4), ("stc", 4))
    whole(0, 640, 4, 5)

    arrive(("tt", "7"))
    across("tt", 5)
    arrive(("tt", "5a"), ("tt", "6a"))
    across("tt", 6)
    arrive(("tt", "5b"), ("tt", "6b"))
    across("tt", 7)
    arrive(*[("ti", part) for part in ("7", "5a", "6a", "5b", "6b")])
    teach(640, 384, 0, 5)
    arrive(("ttc", 5), ("ttc", 6), ("ttc", 7))
    teach(0, 1024, 5, 8)

    arrive(("st", "7"))
    across("st", 5)
    arrive(("st", "5a"), ("st", "6a"))
    across("st", 6)
    arrive(*[("si", part) for part in ("7", "5a", "6a")])
    learn(640, 256, 0, 5)
    arrive(("st", "5b"), ("st", "6b"))
    across("st", 7)
    arrive(("stc", 5), ("stc", 6))
    learn(0, 896, 5, 7)
    arrive(("si", "5b"), ("si", "6b"))
    learn(896, 128, 0, 7)

    def give(slots):
        for p in slots:
            lo = p * 2 * ROWS + ROWS
            tb[p * ROWS : (p + 1) * ROWS] = tacc[lo : lo + ROWS].astype(jnp.bfloat16)
        for p in slots:
            rows = pl.ds(p * ROWS, ROWS)
            got["g", p] = remote(tb.at[rows], crecv.at[rows], csend_g.at[p], crecv_g.at[p], twin)

    give((5, 1, 2, 6, 4, 3, 0))
    arrive(("stc", 7))
    learn(0, 1024, 7, 8)
    give((7,))

    def part_of(p, load):
        if p in (5, 6):
            lo = 0 if p == 5 else HALF
            return ((0, load(6, lo, HALF)), (HALF, load(7, lo, HALF)))
        return ((0, load(5 if p == 7 else p, 0, ROWS)),)

    def img_part(p):
        return part_of(p, lambda slot, lo, count: iacc[slot * ROWS + lo : slot * ROWS + lo + count])

    def txt_part(p):
        def load(slot, lo, count):
            mine = tacc[slot * 2 * ROWS + lo : slot * 2 * ROWS + lo + count]
            return mine + crecv[slot * ROWS + lo : slot * ROWS + lo + count].astype(jnp.float32)

        return part_of(p, load)

    def at(ref, p):
        return ref.at[pl.ds(p * ROWS, ROWS)]

    def fill(ref, p, parts):
        for lo, value in parts:
            ref[p * ROWS + lo : p * ROWS + lo + value.shape[0]] = value.astype(jnp.bfloat16)

    def put_img(p, slot, dev):
        got["i", slot] = remote(at(ib, p), at(irecv, slot), isend.at[slot], irsem.at[slot], dev)

    def put_txt(p, slot, dev):
        got["t", slot] = remote(at(ts, p), at(trecv, slot), tsend.at[slot], trsem.at[slot], dev)

    def came(ref, slot):
        return ref[slot * ROWS : (slot + 1) * ROWS].astype(jnp.float32)

    for p in (7, 5, 6, 1, 2):
        fill(ib, p, img_part(p))
    put_img(7, 0, img_side)
    put_img(5, 1, img_up)
    put_img(6, 2, img_down)
    put_img(1, 3, img_up)
    put_img(2, 4, img_down)
    arrive(*[("g", p) for p in (5, 1, 2)])
    for p in (7, 1, 2):
        fill(ts, p, txt_part(p))
    put_txt(7, 0, txt_side)
    put_txt(1, 3, txt_up)
    put_txt(2, 4, txt_down)
    arrive(*[("g", p) for p in (6, 4, 3, 0, 7)])
    for p in (5, 6):
        fill(ts, p, txt_part(p))
    put_txt(5, 1, txt_up)
    put_txt(6, 2, txt_down)

    arrive(("i", 0))
    ib[4 * ROWS : 5 * ROWS] = (iacc[4 * ROWS : 5 * ROWS] + came(irecv, 0)).astype(jnp.bfloat16)
    put_img(4, 5, img_far)
    arrive(("i", 1), ("i", 2))
    ib[3 * ROWS : 4 * ROWS] = (iacc[3 * ROWS : 4 * ROWS] + came(irecv, 1) + came(irecv, 2)).astype(jnp.bfloat16)
    put_img(3, 6, img_side)
    arrive(("t", 0))
    ts[4 * ROWS : 5 * ROWS] = (txt_part(4)[0][1] + came(trecv, 0)).astype(jnp.bfloat16)
    put_txt(4, 5, txt_far)
    arrive(("t", 1), ("t", 2))
    ts[3 * ROWS : 4 * ROWS] = (txt_part(3)[0][1] + came(trecv, 1) + came(trecv, 2)).astype(jnp.bfloat16)
    put_txt(3, 6, txt_side)

    arrive(*[("i", slot) for slot in (3, 4, 5, 6)])
    total = iacc[0:ROWS] + came(irecv, 3) + came(irecv, 4) + came(irecv, 5) + came(irecv, 6)
    image_grad[...] = back(logit_scale * total, img_raw[...])
    arrive(*[("t", slot) for slot in (3, 4, 5, 6)])
    total = txt_part(0)[0][1] + came(trecv, 3) + came(trecv, 4) + came(trecv, 5) + came(trecv, 6)
    text_grad[...] = back(logit_scale * total, txt_raw[...])

    for copy in sent:
        copy.wait_send()


def body(student_img, student_txt, teacher_img, teacher_txt):
    width = student_img.shape[1]
    t_width = teacher_img.shape[1]
    bf16, f32 = jnp.bfloat16, jnp.float32
    vmem = pl.BlockSpec(memory_space=pltpu.VMEM)
    dma = pltpu.SemaphoreType.DMA((10,))
    return pl.pallas_call(
        kernel,
        out_shape=[jax.ShapeDtypeStruct((ROWS, width), f32)] * 2,
        in_specs=[vmem] * 4,
        out_specs=[vmem] * 2,
        scratch_shapes=[
            pltpu.VMEM((8 * ROWS, width), bf16),
            pltpu.VMEM((8 * ROWS, t_width), bf16),
            pltpu.VMEM((16 * ROWS, width), bf16),
            pltpu.VMEM((16 * ROWS, t_width), bf16),
            pltpu.VMEM((8, 8 * ROWS, 2 * ROWS), f32),
            pltpu.VMEM((8 * ROWS, 2 * ROWS), bf16),
            pltpu.VMEM((8 * ROWS, width), f32),
            pltpu.VMEM((16 * ROWS, width), f32),
            pltpu.VMEM((8 * ROWS, width), bf16),
            pltpu.VMEM((8 * ROWS, width), bf16),
            pltpu.VMEM((8 * ROWS, width), bf16),
            pltpu.VMEM((8 * ROWS, width), bf16),
            pltpu.VMEM((7 * ROWS, width), bf16),
            pltpu.VMEM((7 * ROWS, width), bf16),
        ]
        + [dma] * 18,
        compiler_params=pltpu.CompilerParams(
            collective_id=0, has_side_effects=True, vmem_limit_bytes=62 << 20
        ),
    )(student_img, student_txt, teacher_img, teacher_txt)


def solution(mesh):
    rows = P(("blk", "narrow"), None)
    return jax.shard_map(body, mesh=mesh, in_specs=(rows,) * 4, out_specs=(rows, rows), check_vma=False)
```

```python
import jax
import jax.numpy as jnp
from jax import lax
from jax.experimental import pallas as pl
from jax.experimental.pallas import tpu as pltpu
from jax.sharding import PartitionSpec as P

epsilon = 1e-06
logit_scale = 100.0
logit_bias = -4.0
half_scale = 0.5 * logit_scale
half_bias = 0.5 * logit_bias

ROWS = 128
MESH_ID = pl.DeviceIdType.MESH
NT = (((1,), (1,)), ((), ()))
NN = (((1,), (0,)), ((), ()))
TN = (((0,), (0,)), ((), ()))

HALF = ROWS // 2


def dot(a, b, dims):
    return lax.dot_general(a, b, dims, preferred_element_type=jnp.float32)


def unit_of(raw):
    x = raw.astype(jnp.float32)
    radius = jnp.sqrt(jnp.sum(x * x, axis=1, keepdims=True) + epsilon)
    return x / radius, radius


def back(grad, raw):
    unit, radius = unit_of(raw)
    along = jnp.sum(unit * grad, axis=1, keepdims=True)
    return (grad - unit * along) / radius


def kernel(
    img_raw, txt_raw, timg_raw, ttxt_raw, image_grad, text_grad,
    si, ti, st, tt, pn2, pa2, pn3, pa3, gs, iacc, tacc, ib, tb, ts, crecv, irecv, trecv,
    send_si, send_ti, send_st, send_tt, recv_si, recv_ti, recv_st, recv_tt,
    csend_st, csend_tt, crecv_st, crecv_tt, csend_g, crecv_g, isend, irsem, tsend, trsem,
):
    b = lax.axis_index("blk")
    n = lax.axis_index("narrow")
    core = lax.rem(b, 2)
    z = b // 4
    x = 2 * lax.rem(b // 2, 2) + n // 4
    y = lax.rem(n, 4)
    odd = lax.rem(x, 2)

    def device(x, y, z, core):
        return ((z * 2 + x // 2) * 2 + core, lax.rem(x, 2) * 4 + y)

    def step(v, by):
        return lax.rem(v + 4 + by, 4)

    x_img = x + 1 - 2 * odd
    x_txt = lax.rem(x + 3 + 2 * odd, 4)
    img_up = device(x, step(y, 1), z, core)
    img_down = device(x, step(y, -1), z, core)
    img_far = device(x, step(y, 2), z, core)
    img_side = device(x_img, y, z, core)
    txt_up = device(x, y, step(z, 1), core)
    txt_down = device(x, y, step(z, -1), core)
    txt_far = device(x, y, step(z, 2), core)
    txt_side = device(x_txt, y, z, core)
    twin = device(x, y, z, 1 - core)

    barrier = pltpu.get_barrier_semaphore()
    for peer in (img_up, img_down, img_far, img_side, txt_up, txt_down, txt_far, txt_side, twin):
        pl.semaphore_signal(barrier, inc=1, device_id=peer, device_id_type=MESH_ID)

    ti[0:ROWS] = unit_of(timg_raw[...])[0].astype(jnp.bfloat16)
    tt[0:ROWS] = unit_of(ttxt_raw[...])[0].astype(jnp.bfloat16)

    pl.semaphore_wait(barrier, 9)

    sent = []

    def remote(src, dst, ssem, rsem, dev):
        copy = pltpu.make_async_remote_copy(
            src_ref=src, dst_ref=dst, send_sem=ssem, recv_sem=rsem, device_id=dev, device_id_type=MESH_ID
        )
        copy.start()
        sent.append(copy)
        return copy

    img_devs = (img_up, img_down, img_side)
    txt_devs = (txt_up, txt_down, txt_side)
    arrays = {
        "ti": (ti, send_ti, recv_ti, ROWS, img_devs),
        "si": (si, send_si, recv_si, ROWS, img_devs),
        "tt": (tt, send_tt, recv_tt, 2 * ROWS, txt_devs),
        "st": (st, send_st, recv_st, 2 * ROWS, txt_devs),
    }
    got = {}
    UP, DOWN, SIDE = 0, 1, 2
    slot_of = {"0": 0, "1": 1, "2": 2, "3": 3, "4": 4, "7": 5, "5": 6, "6": 7}
    places = {}
    for chip, slot in slot_of.items():
        places[chip] = (slot, 0, ROWS)
        places[chip + "a"] = (slot, 0, HALF)
        places[chip + "b"] = (slot, HALF, HALF)
    index = {k: i for i, k in enumerate(("1a", "1b", "2a", "2b", "3", "4a", "4b", "7", "5", "6"))}

    def hop(name, src, dst, way):
        ref, ssem, rsem, pitch, devs = arrays[name]
        s_slot, s_row, count = places[src]
        d_slot, d_row, _ = places[dst]
        got[name, dst] = remote(
            ref.at[pl.ds(s_slot * pitch + s_row, count)], ref.at[pl.ds(d_slot * pitch + d_row, count)],
            ssem.at[index[dst]], rsem.at[index[dst]], devs[way],
        )

    def across(name, slot):
        ref, _, _, pitch, _ = arrays[name]
        ssem, rsem = (csend_tt, crecv_tt) if name == "tt" else (csend_st, crecv_st)
        got[name + "c", slot] = remote(
            ref.at[pl.ds(slot * pitch, ROWS)], ref.at[pl.ds(slot * pitch + ROWS, ROWS)],
            ssem.at[slot], rsem.at[slot], twin,
        )

    def arrive(*keys):
        for key in keys:
            got[key].wait_recv()

    def to_ring_first(names):
        for name in names:
            hop(name, "0a", "2a", UP)
            hop(name, "0b", "1b", DOWN)
        for name in names:
            hop(name, "0b", "2b", UP)
            hop(name, "0a", "1a", DOWN)

    def to_side_first(names):
        for name in names:
            hop(name, "0", "3", SIDE)
        across(names[1], 0)

    to_ring_first(("ti", "tt"))
    to_side_first(("ti", "tt"))
    si[0:ROWS] = unit_of(img_raw[...])[0].astype(jnp.bfloat16)
    st[0:ROWS] = unit_of(txt_raw[...])[0].astype(jnp.bfloat16)
    to_side_first(("si", "st"))

    def clear(i, _):
        rows = pl.ds(pl.multiple_of(i * ROWS, ROWS), ROWS)
        iacc[rows, :] = jnp.zeros((ROWS, iacc.shape[1]), jnp.float32)
        tacc[pl.ds(pl.multiple_of(i * 2 * ROWS, 2 * ROWS), 2 * ROWS), :] = jnp.zeros(
            (2 * ROWS, tacc.shape[1]), jnp.float32
        )
        return 0

    lax.fori_loop(0, 8, clear, 0)

    def teacher_value(zt):
        return 0.5 - 0.5 * jnp.tanh(half_scale * zt + half_bias)

    WIDE = 4 * ROWS

    def columns(pair):
        return pl.ds(pl.multiple_of(pair * WIDE, WIDE), WIDE)

    def teach(first, count, pair):
        return teacher_value(dot(ti[first : first + count], tt[columns(pair), :], NT))

    def learn(first, count, pair, teacher, diagonal=False):
        rows = slice(first, first + count)
        cols = columns(pair)
        value = jnp.tanh(half_scale * dot(si[rows], st[cols, :], NT) + half_bias) + teacher
        if diagonal:
            row = lax.broadcasted_iota(jnp.int32, (ROWS, WIDE), 0)
            col = lax.broadcasted_iota(jnp.int32, (ROWS, WIDE), 1)
            positive = jnp.where(row == col + pair * WIDE, 1.0, 0.0)
            gs[0:ROWS] = (value[:ROWS] - positive).astype(jnp.bfloat16)
            gs[ROWS:count] = value[ROWS:].astype(jnp.bfloat16)
        else:
            gs[0:count] = value.astype(jnp.bfloat16)
        g = gs[0:count]
        iacc[rows] += dot(g, st[cols, :], NN)
        tacc[cols, :] += dot(g, si[rows], TN)

    def over(begin, end, one):
        lax.fori_loop(begin, end, lambda pair, _: (one(pair), 0)[1], 0)

    def relay(names):
        arrive(*[(name, part) for part in ("2a", "1b") for name in names])
        for name in names:
            hop(name, "2a", "4a", UP)
            hop(name, "1b", "4b", DOWN)

    def to_ring(names):
        for name in names:
            hop(name, "3", "6", UP)
            hop(name, "3", "5", DOWN)

    def near_across(names):
        arrive(*[(name, part) for part in ("2b", "1a", "3") for name in names])
        for slot in (1, 2, 3):
            across(names[1], slot)

    def far_to_side(names):
        arrive(*[(name, part) for part in ("4a", "4b") for name in names])
        for name in names:
            hop(name, "4", "7", SIDE)
        across(names[1], 4)

    def late_across(name, chips):
        for chip in chips:
            arrive((name, chip))
            across(name, slot_of[chip])

    TEACHER, STUDENT = ("ti", "tt"), ("si", "st")
    relay(TEACHER)
    to_ring_first(STUDENT)
    near_across(TEACHER)
    far_to_side(TEACHER)
    relay(STUDENT)
    to_ring(TEACHER)
    near_across(STUDENT)
    to_ring(STUDENT)

    arrive(*[(name, slot) for slot in range(4) for name in ("ttc", "stc")])
    learn(0, 512, 0, teach(0, 512, 0), True)
    far_to_side(STUDENT)
    learn(0, 512, 1, teach(0, 512, 1))

    late_across("tt", "7")
    arrive(("ti", "7"))

    def teach_new2(pair):
        pn2[pair] = teach(512, 256, pair)

    over(0, 2, teach_new2)
    arrive(("ttc", 4), ("ttc", 5))
    pa2[...] = teach(0, 768, 2)

    late_across("st", "7")
    arrive(("si", "7"))
    over(0, 2, lambda pair: learn(512, 256, pair, pn2[pair]))
    arrive(("stc", 4), ("stc", 5))
    learn(0, 768, 2, pa2[...])

    late_across("tt", "56")
    arrive(("ti", "5"), ("ti", "6"))

    def teach_new3(pair):
        pn3[pair] = teach(768, 256, pair)

    over(0, 3, teach_new3)
    arrive(("ttc", 6), ("ttc", 7))
    pa3[...] = teach(0, 1024, 3)

    late_across("st", "56")
    arrive(("si", "5"), ("si", "6"))
    over(0, 3, lambda pair: learn(768, 256, pair, pn3[pair]))

    def give(slots):
        for p in slots:
            lo = p * 2 * ROWS + ROWS
            tb[p * ROWS : (p + 1) * ROWS] = tacc[lo : lo + ROWS].astype(jnp.bfloat16)
        for p in slots:
            rows = pl.ds(p * ROWS, ROWS)
            got["g", p] = remote(tb.at[rows], crecv.at[rows], csend_g.at[p], crecv_g.at[p], twin)

    give((5, 1, 2, 4, 3, 0))
    arrive(("stc", 6), ("stc", 7))
    learn(0, 1024, 3, pa3[...])
    give((6, 7))

    def img_part(p):
        slot = slot_of[str(p)]
        return iacc[slot * ROWS : (slot + 1) * ROWS]

    def txt_part(p):
        slot = slot_of[str(p)]
        mine = tacc[slot * 2 * ROWS : slot * 2 * ROWS + ROWS]
        return mine + crecv[slot * ROWS : (slot + 1) * ROWS].astype(jnp.float32)

    def at(ref, p):
        return ref.at[pl.ds(p * ROWS, ROWS)]

    def fill(ref, p, value):
        ref[p * ROWS : (p + 1) * ROWS] = value.astype(jnp.bfloat16)

    def put_img(p, slot, dev):
        got["i", slot] = remote(at(ib, p), at(irecv, slot), isend.at[slot], irsem.at[slot], dev)

    def put_txt(p, slot, dev):
        got["t", slot] = remote(at(ts, p), at(trecv, slot), tsend.at[slot], trsem.at[slot], dev)

    def came(ref, slot):
        return ref[slot * ROWS : (slot + 1) * ROWS].astype(jnp.float32)

    for p in (7, 5, 6, 1, 2):
        fill(ib, p, img_part(p))
    put_img(7, 0, img_side)
    put_img(5, 1, img_up)
    put_img(6, 2, img_down)
    put_img(1, 3, img_up)
    put_img(2, 4, img_down)
    arrive(*[("g", p) for p in (5, 1, 2)])
    for p in (7, 1, 2):
        fill(ts, p, txt_part(p))
    put_txt(7, 0, txt_side)
    put_txt(1, 3, txt_up)
    put_txt(2, 4, txt_down)
    arrive(*[("g", p) for p in (4, 3, 0, 6, 7)])
    for p in (5, 6):
        fill(ts, p, txt_part(p))
    put_txt(5, 1, txt_up)
    put_txt(6, 2, txt_down)

    arrive(("i", 0))
    ib[4 * ROWS : 5 * ROWS] = (iacc[4 * ROWS : 5 * ROWS] + came(irecv, 0)).astype(jnp.bfloat16)
    put_img(4, 5, img_far)
    arrive(("i", 1), ("i", 2))
    ib[3 * ROWS : 4 * ROWS] = (iacc[3 * ROWS : 4 * ROWS] + came(irecv, 1) + came(irecv, 2)).astype(jnp.bfloat16)
    put_img(3, 6, img_side)
    arrive(("t", 0))
    ts[4 * ROWS : 5 * ROWS] = (txt_part(4) + came(trecv, 0)).astype(jnp.bfloat16)
    put_txt(4, 5, txt_far)
    arrive(("t", 1), ("t", 2))
    ts[3 * ROWS : 4 * ROWS] = (txt_part(3) + came(trecv, 1) + came(trecv, 2)).astype(jnp.bfloat16)
    put_txt(3, 6, txt_side)

    arrive(*[("i", slot) for slot in (3, 4, 5, 6)])
    total = iacc[0:ROWS] + came(irecv, 3) + came(irecv, 4) + came(irecv, 5) + came(irecv, 6)
    image_grad[...] = back(logit_scale * total, img_raw[...])
    arrive(*[("t", slot) for slot in (3, 4, 5, 6)])
    total = txt_part(0) + came(trecv, 3) + came(trecv, 4) + came(trecv, 5) + came(trecv, 6)
    text_grad[...] = back(logit_scale * total, txt_raw[...])

    for copy in sent:
        copy.wait_send()


def body(student_img, student_txt, teacher_img, teacher_txt):
    width = student_img.shape[1]
    t_width = teacher_img.shape[1]
    bf16, f32 = jnp.bfloat16, jnp.float32
    vmem = pl.BlockSpec(memory_space=pltpu.VMEM)
    dma = pltpu.SemaphoreType.DMA((10,))
    return pl.pallas_call(
        kernel,
        out_shape=[jax.ShapeDtypeStruct((ROWS, width), f32)] * 2,
        in_specs=[vmem] * 4,
        out_specs=[vmem] * 2,
        scratch_shapes=[
            pltpu.VMEM((8 * ROWS, width), bf16),
            pltpu.VMEM((8 * ROWS, t_width), bf16),
            pltpu.VMEM((16 * ROWS, width), bf16),
            pltpu.VMEM((16 * ROWS, t_width), bf16),
            pltpu.VMEM((2, 2 * ROWS, 4 * ROWS), f32),
            pltpu.VMEM((6 * ROWS, 4 * ROWS), f32),
            pltpu.VMEM((3, 2 * ROWS, 4 * ROWS), f32),
            pltpu.VMEM((8 * ROWS, 4 * ROWS), f32),
            pltpu.VMEM((8 * ROWS, 4 * ROWS), bf16),
            pltpu.VMEM((8 * ROWS, width), f32),
            pltpu.VMEM((16 * ROWS, width), f32),
            pltpu.VMEM((8 * ROWS, width), bf16),
            pltpu.VMEM((8 * ROWS, width), bf16),
            pltpu.VMEM((8 * ROWS, width), bf16),
            pltpu.VMEM((8 * ROWS, width), bf16),
            pltpu.VMEM((7 * ROWS, width), bf16),
            pltpu.VMEM((7 * ROWS, width), bf16),
        ]
        + [dma] * 18,
        compiler_params=pltpu.CompilerParams(
            collective_id=0, has_side_effects=True, vmem_limit_bytes=62 << 20
        ),
    )(student_img, student_txt, teacher_img, teacher_txt)


def solution(mesh):
    rows = P(("blk", "narrow"), None)
    return jax.shard_map(body, mesh=mesh, in_specs=(rows,) * 4, out_specs=(rows, rows), check_vma=False)
```

```python
import jax
import jax.numpy as jnp
from jax import lax
from jax.experimental import pallas as pl
from jax.experimental.pallas import tpu as pltpu
from jax.sharding import PartitionSpec as P

epsilon = 1e-06
logit_scale = 100.0
logit_bias = -4.0
half_scale = 0.5 * logit_scale
half_bias = 0.5 * logit_bias

ROWS = 128
MESH_ID = pl.DeviceIdType.MESH
NT = (((1,), (1,)), ((), ()))
NN = (((1,), (0,)), ((), ()))
TN = (((0,), (0,)), ((), ()))

HALF = ROWS // 2


def dot(a, b, dims):
    return lax.dot_general(a, b, dims, preferred_element_type=jnp.float32)


def unit_of(raw):
    x = raw.astype(jnp.float32)
    radius = jnp.sqrt(jnp.sum(x * x, axis=1, keepdims=True) + epsilon)
    return x / radius, radius


def back(grad, raw):
    unit, radius = unit_of(raw)
    along = jnp.sum(unit * grad, axis=1, keepdims=True)
    return (grad - unit * along) / radius


def kernel(
    img_hbm, txt_hbm, timg_hbm, ttxt_hbm, image_grad, text_grad, img_raw, txt_raw, timg_raw, ttxt_raw,
    si, ti, st, tt, pn2, pa2, pn3, pa3, gs, iacc, tacc, ib, tb, ts, crecv, irecv, trecv,
    send_si, send_ti, send_st, send_tt, recv_si, recv_ti, recv_st, recv_tt,
    csend_st, csend_tt, crecv_st, crecv_tt, csend_g, crecv_g, load, isend, irsem, tsend, trsem,
):
    b = lax.axis_index("blk")
    n = lax.axis_index("narrow")
    core = lax.rem(b, 2)
    z = b // 4
    x = 2 * lax.rem(b // 2, 2) + n // 4
    y = lax.rem(n, 4)
    odd = lax.rem(x, 2)

    def device(x, y, z, core):
        return ((z * 2 + x // 2) * 2 + core, lax.rem(x, 2) * 4 + y)

    def step(v, by):
        return lax.rem(v + 4 + by, 4)

    x_img = x + 1 - 2 * odd
    x_txt = lax.rem(x + 3 + 2 * odd, 4)
    img_up = device(x, step(y, 1), z, core)
    img_down = device(x, step(y, -1), z, core)
    img_side = device(x_img, y, z, core)
    txt_up = device(x, y, step(z, 1), core)
    txt_down = device(x, y, step(z, -1), core)
    txt_side = device(x_txt, y, z, core)
    twin = device(x, y, z, 1 - core)

    barrier = pltpu.get_barrier_semaphore()
    for peer in (img_up, img_down, img_side, txt_up, txt_down, txt_side, twin):
        pl.semaphore_signal(barrier, inc=1, device_id=peer, device_id_type=MESH_ID)

    loads = [
        pltpu.make_async_copy(src, dst, load.at[i])
        for i, (src, dst) in enumerate(
            ((timg_hbm, timg_raw), (ttxt_hbm, ttxt_raw), (img_hbm, img_raw), (txt_hbm, txt_raw))
        )
    ]
    for copy in loads:
        copy.start()
    for copy in loads[:2]:
        copy.wait()
    ti[0:ROWS] = unit_of(timg_raw[...])[0].astype(jnp.bfloat16)
    tt[0:ROWS] = unit_of(ttxt_raw[...])[0].astype(jnp.bfloat16)

    pl.semaphore_wait(barrier, 7)

    sent = []

    def remote(src, dst, ssem, rsem, dev):
        copy = pltpu.make_async_remote_copy(
            src_ref=src, dst_ref=dst, send_sem=ssem, recv_sem=rsem, device_id=dev, device_id_type=MESH_ID
        )
        copy.start()
        sent.append(copy)
        return copy

    img_devs = (img_up, img_down, img_side)
    txt_devs = (txt_up, txt_down, txt_side)
    arrays = {
        "ti": (ti, send_ti, recv_ti, ROWS, img_devs),
        "si": (si, send_si, recv_si, ROWS, img_devs),
        "tt": (tt, send_tt, recv_tt, 2 * ROWS, txt_devs),
        "st": (st, send_st, recv_st, 2 * ROWS, txt_devs),
    }
    got = {}
    UP, DOWN, SIDE = 0, 1, 2
    slot_of = {"0": 0, "3": 1, "1": 2, "2": 3, "4": 4, "7": 5, "5": 6, "6": 7}
    places = {}
    for chip, slot in slot_of.items():
        places[chip] = (slot, 0, ROWS)
        places[chip + "a"] = (slot, 0, HALF)
        places[chip + "b"] = (slot, HALF, HALF)
    index = {k: i for i, k in enumerate(("1a", "1b", "2a", "2b", "3", "4a", "4b", "7", "5", "6"))}

    def hop(name, src, dst, way):
        ref, ssem, rsem, pitch, devs = arrays[name]
        s_slot, s_row, count = places[src]
        d_slot, d_row, _ = places[dst]
        got[name, dst] = remote(
            ref.at[pl.ds(s_slot * pitch + s_row, count)], ref.at[pl.ds(d_slot * pitch + d_row, count)],
            ssem.at[index[dst]], rsem.at[index[dst]], devs[way],
        )

    def across(name, slot):
        ref, _, _, pitch, _ = arrays[name]
        ssem, rsem = (csend_tt, crecv_tt) if name == "tt" else (csend_st, crecv_st)
        got[name + "c", slot] = remote(
            ref.at[pl.ds(slot * pitch, ROWS)], ref.at[pl.ds(slot * pitch + ROWS, ROWS)],
            ssem.at[slot], rsem.at[slot], twin,
        )

    def arrive(*keys):
        for key in keys:
            got[key].wait_recv()

    def to_ring_first(names):
        for name in names:
            hop(name, "0a", "2a", UP)
            hop(name, "0b", "1b", DOWN)
        for name in names:
            hop(name, "0b", "2b", UP)
            hop(name, "0a", "1a", DOWN)

    def to_side_first(names):
        for name in names:
            hop(name, "0", "3", SIDE)
        across(names[1], 0)

    to_ring_first(("ti", "tt"))
    to_side_first(("ti", "tt"))
    for copy in loads[2:]:
        copy.wait()
    si[0:ROWS] = unit_of(img_raw[...])[0].astype(jnp.bfloat16)
    st[0:ROWS] = unit_of(txt_raw[...])[0].astype(jnp.bfloat16)
    to_side_first(("si", "st"))

    def clear(i, _):
        rows = pl.ds(pl.multiple_of(i * ROWS, ROWS), ROWS)
        iacc[rows, :] = jnp.zeros((ROWS, iacc.shape[1]), jnp.float32)
        tacc[pl.ds(pl.multiple_of(i * 2 * ROWS, 2 * ROWS), 2 * ROWS), :] = jnp.zeros(
            (2 * ROWS, tacc.shape[1]), jnp.float32
        )
        return 0

    lax.fori_loop(0, 8, clear, 0)

    def teacher_value(zt):
        return 0.5 - 0.5 * jnp.tanh(half_scale * zt + half_bias)

    WIDE = 4 * ROWS

    def columns(pair):
        return pl.ds(pl.multiple_of(pair * WIDE, WIDE), WIDE)

    def teach(first, count, pair):
        return teacher_value(dot(ti[first : first + count], tt[columns(pair), :], NT))

    def learn(first, count, pair, teacher, diagonal=False):
        rows = slice(first, first + count)
        cols = columns(pair)
        value = jnp.tanh(half_scale * dot(si[rows], st[cols, :], NT) + half_bias) + teacher
        if diagonal:
            row = lax.broadcasted_iota(jnp.int32, (ROWS, WIDE), 0)
            col = lax.broadcasted_iota(jnp.int32, (ROWS, WIDE), 1)
            positive = jnp.where(row == col + pair * WIDE, 1.0, 0.0)
            gs[0:ROWS] = (value[:ROWS] - positive).astype(jnp.bfloat16)
            gs[ROWS:count] = value[ROWS:].astype(jnp.bfloat16)
        else:
            gs[0:count] = value.astype(jnp.bfloat16)
        g = gs[0:count]
        iacc[rows] += dot(g, st[cols, :], NN)
        tacc[cols, :] += dot(g, si[rows], TN)

    def over(begin, end, one):
        lax.fori_loop(begin, end, lambda pair, _: (one(pair), 0)[1], 0)

    def relay(names):
        arrive(*[(name, part) for part in ("2a", "1b") for name in names])
        for name in names:
            hop(name, "2a", "4a", UP)
            hop(name, "1b", "4b", DOWN)

    def to_ring(names):
        for name in names:
            hop(name, "3", "6", UP)
            hop(name, "3", "5", DOWN)

    def near_across(names):
        arrive(*[(name, part) for part in ("2b", "1a", "3") for name in names])
        for slot in (1, 2, 3):
            across(names[1], slot)

    def far_to_side(names):
        arrive(*[(name, part) for part in ("4a", "4b") for name in names])
        for name in names:
            hop(name, "4", "7", SIDE)
        across(names[1], slot_of["4"])

    def late_across(name, chips):
        for chip in chips:
            arrive((name, chip))
            across(name, slot_of[chip])

    TEACHER, STUDENT = ("ti", "tt"), ("si", "st")
    relay(TEACHER)
    to_ring_first(STUDENT)
    near_across(TEACHER)
    far_to_side(TEACHER)
    relay(STUDENT)
    to_ring(TEACHER)
    near_across(STUDENT)
    to_ring(STUDENT)

    arrive(*[(name, slot) for slot in range(4) for name in ("ttc", "stc")])
    learn(0, 512, 0, teach(0, 512, 0), True)
    far_to_side(STUDENT)
    learn(0, 512, 1, teach(0, 512, 1))

    late_across("tt", "7")
    arrive(("ti", "7"))

    def teach_new2(pair):
        pn2[pair] = teach(512, 256, pair)

    over(0, 2, teach_new2)
    arrive(("ttc", 4), ("ttc", 5))
    pa2[...] = teach(0, 768, 2)

    late_across("st", "7")
    arrive(("si", "7"))
    over(0, 2, lambda pair: learn(512, 256, pair, pn2[pair]))
    arrive(("stc", 4), ("stc", 5))
    learn(0, 768, 2, pa2[...])

    late_across("tt", "56")
    arrive(("ti", "5"), ("ti", "6"))

    def teach_new3(pair):
        pn3[pair] = teach(768, 256, pair)

    over(0, 3, teach_new3)
    arrive(("ttc", 6), ("ttc", 7))
    pa3[...] = teach(0, 1024, 3)

    late_across("st", "56")
    arrive(("si", "5"), ("si", "6"))
    def give(slots):
        for p in slots:
            lo = p * 2 * ROWS + ROWS
            tb[p * ROWS : (p + 1) * ROWS] = tacc[lo : lo + ROWS].astype(jnp.bfloat16)
        for p in slots:
            rows = pl.ds(p * ROWS, ROWS)
            got["g", p] = remote(tb.at[rows], crecv.at[rows], csend_g.at[p], crecv_g.at[p], twin)

    def img_part(chip):
        slot = slot_of[chip]
        return iacc[slot * ROWS : (slot + 1) * ROWS]

    def txt_part(chip):
        slot = slot_of[chip]
        mine = tacc[slot * 2 * ROWS : slot * 2 * ROWS + ROWS]
        return mine + crecv[slot * ROWS : (slot + 1) * ROWS].astype(jnp.float32)

    part = {"i": img_part, "t": txt_part}
    out_buf = {"i": ib, "t": ts}
    in_buf = {"i": irecv, "t": trecv}
    out_sem = {"i": isend, "t": tsend}
    in_sem = {"i": irsem, "t": trsem}
    peers = {"i": img_devs, "t": txt_devs}
    piece = {"1": (0, ROWS, 0), "2": (ROWS, ROWS, 1), "3": (2 * ROWS, ROWS, 2), "4": (3 * ROWS, ROWS, 3),
             "5": (4 * ROWS, ROWS, 4), "6": (5 * ROWS, ROWS, 5), "7": (6 * ROWS, ROWS, 6)}
    for chip, first_sem in (("1", 0), ("2", 1), ("4", 3)):
        row = piece[chip][0]
        piece[chip + "a"] = (row, HALF, first_sem)
        piece[chip + "b"] = (row + HALF, HALF, first_sem + 7 if chip != "4" else 9)

    def rows_of(ref, key):
        row, count, _ = piece[key]
        return ref[row : row + count]

    def fill(stream, key, value):
        row, count, _ = piece[key]
        out_buf[stream][row : row + count] = value.astype(jnp.bfloat16)

    def put(stream, key, way):
        row, count, sem = piece[key]
        rows = pl.ds(row, count)
        got[stream, "sum" + key] = remote(
            out_buf[stream].at[rows], in_buf[stream].at[rows],
            out_sem[stream].at[sem], in_sem[stream].at[sem], peers[stream][way],
        )

    def came(stream, key):
        arrive((stream, "sum" + key))
        return rows_of(in_buf[stream], key).astype(jnp.float32)

    def send_7(stream):
        fill(stream, "7", part[stream]("7"))
        put(stream, "7", SIDE)

    def send_near(stream):
        fill(stream, "1", part[stream]("1"))
        fill(stream, "2", part[stream]("2"))
        put(stream, "1a", UP)
        put(stream, "2b", DOWN)

    def send_56(stream):
        fill(stream, "5", part[stream]("5"))
        fill(stream, "6", part[stream]("6"))
        put(stream, "5", UP)
        put(stream, "6", DOWN)

    def send_far(stream):
        fill(stream, "4", part[stream]("4") + came(stream, "7"))
        put(stream, "4b", UP)
        put(stream, "4a", DOWN)

    def send_side(stream):
        fill(stream, "3", part[stream]("3") + came(stream, "5") + came(stream, "6"))
        put(stream, "3", SIDE)

    def send_rest(stream):
        fill(stream, "1b", part[stream]("1")[HALF:] + came(stream, "4b"))
        fill(stream, "2a", part[stream]("2")[:HALF] + came(stream, "4a"))
        put(stream, "1b", UP)
        put(stream, "2a", DOWN)

    def total(stream):
        for key in ("1a", "1b", "2a", "2b"):
            arrive((stream, "sum" + key))
        near = rows_of(in_buf[stream], "1").astype(jnp.float32) + rows_of(in_buf[stream], "2").astype(jnp.float32)
        return logit_scale * (part[stream]("0") + near + came(stream, "3"))

    learn(768, 256, 2, pn3[2])
    give((5, 4))
    learn(768, 256, 1, pn3[1])
    give((2, 3))
    arrive(("stc", 6), ("stc", 7))
    learn(512, 256, 3, pa3[512:768])
    arrive(("g", 5))
    send_7("i")
    send_7("t")
    learn(0, 512, 3, pa3[0:512])
    send_near("i")
    arrive(("g", 2), ("g", 3))
    send_near("t")
    learn(768, 256, 3, pa3[768:1024])
    give((6, 7))
    learn(768, 256, 0, pn3[0])
    send_56("i")
    arrive(("g", 6), ("g", 7))
    send_56("t")
    give((1, 0))
    arrive(("g", 4))
    send_far("i")
    send_far("t")
    arrive(("g", 1))
    send_side("i")
    send_side("t")
    send_rest("i")
    send_rest("t")
    image_grad[...] = back(total("i"), img_raw[...])
    arrive(("g", 0))
    text_grad[...] = back(total("t"), txt_raw[...])

    for copy in sent:
        copy.wait_send()


def body(student_img, student_txt, teacher_img, teacher_txt):
    width = student_img.shape[1]
    t_width = teacher_img.shape[1]
    bf16, f32 = jnp.bfloat16, jnp.float32
    vmem = pl.BlockSpec(memory_space=pltpu.VMEM)
    dma = pltpu.SemaphoreType.DMA((10,))
    return pl.pallas_call(
        kernel,
        out_shape=[jax.ShapeDtypeStruct((ROWS, width), f32)] * 2,
        in_specs=[pl.BlockSpec(memory_space=pl.ANY)] * 4,
        out_specs=[vmem] * 2,
        scratch_shapes=[
            pltpu.VMEM((ROWS, width), bf16),
            pltpu.VMEM((ROWS, width), bf16),
            pltpu.VMEM((ROWS, t_width), bf16),
            pltpu.VMEM((ROWS, t_width), bf16),
            pltpu.VMEM((8 * ROWS, width), bf16),
            pltpu.VMEM((8 * ROWS, t_width), bf16),
            pltpu.VMEM((16 * ROWS, width), bf16),
            pltpu.VMEM((16 * ROWS, t_width), bf16),
            pltpu.VMEM((2, 2 * ROWS, 4 * ROWS), f32),
            pltpu.VMEM((6 * ROWS, 4 * ROWS), f32),
            pltpu.VMEM((3, 2 * ROWS, 4 * ROWS), f32),
            pltpu.VMEM((8 * ROWS, 4 * ROWS), f32),
            pltpu.VMEM((8 * ROWS, 4 * ROWS), bf16),
            pltpu.VMEM((8 * ROWS, width), f32),
            pltpu.VMEM((16 * ROWS, width), f32),
            pltpu.VMEM((8 * ROWS, width), bf16),
            pltpu.VMEM((8 * ROWS, width), bf16),
            pltpu.VMEM((8 * ROWS, width), bf16),
            pltpu.VMEM((8 * ROWS, width), bf16),
            pltpu.VMEM((7 * ROWS, width), bf16),
            pltpu.VMEM((7 * ROWS, width), bf16),
        ]
        + [dma] * 19,
        compiler_params=pltpu.CompilerParams(
            collective_id=0, has_side_effects=True, vmem_limit_bytes=62 << 20
        ),
    )(student_img, student_txt, teacher_img, teacher_txt)


def solution(mesh):
    rows = P(("blk", "narrow"), None)
    return jax.shard_map(body, mesh=mesh, in_specs=(rows,) * 4, out_specs=(rows, rows), check_vma=False)
```

```python
import jax
import jax.numpy as jnp
from jax import lax
from jax.experimental import pallas as pl
from jax.experimental.pallas import tpu as pltpu
from jax.sharding import PartitionSpec as P

epsilon = 1e-06
logit_scale = 100.0
logit_bias = -4.0
half_scale = 0.5 * logit_scale
half_bias = 0.5 * logit_bias

ROWS = 128
MESH_ID = pl.DeviceIdType.MESH
NT = (((1,), (1,)), ((), ()))
NN = (((1,), (0,)), ((), ()))
TN = (((0,), (0,)), ((), ()))

HALF = ROWS // 2


def dot(a, b, dims):
    return lax.dot_general(a, b, dims, preferred_element_type=jnp.float32)


def unit_of(raw):
    x = raw.astype(jnp.float32)
    radius = jnp.sqrt(jnp.sum(x * x, axis=1, keepdims=True) + epsilon)
    return x / radius, radius


def back(grad, raw):
    unit, radius = unit_of(raw)
    along = jnp.sum(unit * grad, axis=1, keepdims=True)
    return (grad - unit * along) / radius


def kernel(
    img_hbm, txt_hbm, timg_hbm, ttxt_hbm, grads, img_raw, txt_raw, timg_raw, ttxt_raw,
    si, ti, st, tt, pa1, pn2, pa2, pn3, pa3, gs, iacc, tacc, ib, tb, ts, crecv, irecv, trecv,
    send_si, send_ti, send_st, send_tt, recv_si, recv_ti, recv_st, recv_tt,
    csend_st, csend_tt, crecv_st, crecv_tt, csend_g, crecv_g, load, isend, irsem, tsend, trsem,
):
    b = lax.axis_index("blk")
    n = lax.axis_index("narrow")
    core = lax.rem(b, 2)
    z = b // 4
    x = 2 * lax.rem(b // 2, 2) + n // 4
    y = lax.rem(n, 4)
    odd = lax.rem(x, 2)

    def device(x, y, z, core):
        return ((z * 2 + x // 2) * 2 + core, lax.rem(x, 2) * 4 + y)

    def step(v, by):
        return lax.rem(v + 4 + by, 4)

    x_img = x + 1 - 2 * odd
    x_txt = lax.rem(x + 3 + 2 * odd, 4)
    img_up = device(x, step(y, 1), z, core)
    img_down = device(x, step(y, -1), z, core)
    img_side = device(x_img, y, z, core)
    txt_up = device(x, y, step(z, 1), core)
    txt_down = device(x, y, step(z, -1), core)
    txt_side = device(x_txt, y, z, core)
    twin = device(x, y, z, 1 - core)

    barrier = pltpu.get_barrier_semaphore()
    for peer in (img_up, img_down, img_side, txt_up, txt_down, txt_side, twin):
        pl.semaphore_signal(barrier, inc=1, device_id=peer, device_id_type=MESH_ID)

    loads = [
        pltpu.make_async_copy(src, dst, load.at[i])
        for i, (src, dst) in enumerate(
            ((timg_hbm, timg_raw), (ttxt_hbm, ttxt_raw), (img_hbm, img_raw), (txt_hbm, txt_raw))
        )
    ]
    for copy in loads:
        copy.start()
    for copy in loads[:2]:
        copy.wait()
    ti[0:ROWS] = unit_of(timg_raw[...])[0].astype(jnp.bfloat16)
    tt[0:ROWS] = unit_of(ttxt_raw[...])[0].astype(jnp.bfloat16)

    pl.semaphore_wait(barrier, 7)

    sent = []

    def remote(src, dst, ssem, rsem, dev):
        copy = pltpu.make_async_remote_copy(
            src_ref=src, dst_ref=dst, send_sem=ssem, recv_sem=rsem, device_id=dev, device_id_type=MESH_ID
        )
        copy.start()
        sent.append(copy)
        return copy

    img_devs = (img_up, img_down, img_side)
    txt_devs = (txt_up, txt_down, txt_side)
    arrays = {
        "ti": (ti, send_ti, recv_ti, ROWS, img_devs),
        "si": (si, send_si, recv_si, ROWS, img_devs),
        "tt": (tt, send_tt, recv_tt, 2 * ROWS, txt_devs),
        "st": (st, send_st, recv_st, 2 * ROWS, txt_devs),
    }
    got = {}
    UP, DOWN, SIDE = 0, 1, 2
    slot_of = {"0": 0, "3": 1, "1": 2, "2": 3, "4": 4, "7": 5, "5": 6, "6": 7}
    places = {}
    for chip, slot in slot_of.items():
        places[chip] = (slot, 0, ROWS)
        places[chip + "a"] = (slot, 0, HALF)
        places[chip + "b"] = (slot, HALF, HALF)
    index = {k: i for i, k in enumerate(("1a", "1b", "2a", "2b", "3", "4a", "4b", "7", "5", "6"))}

    def hop(name, src, dst, way):
        ref, ssem, rsem, pitch, devs = arrays[name]
        s_slot, s_row, count = places[src]
        d_slot, d_row, _ = places[dst]
        got[name, dst] = remote(
            ref.at[pl.ds(s_slot * pitch + s_row, count)], ref.at[pl.ds(d_slot * pitch + d_row, count)],
            ssem.at[index[dst]], rsem.at[index[dst]], devs[way],
        )

    def across(name, slot):
        ref, _, _, pitch, _ = arrays[name]
        ssem, rsem = (csend_tt, crecv_tt) if name == "tt" else (csend_st, crecv_st)
        got[name + "c", slot] = remote(
            ref.at[pl.ds(slot * pitch, ROWS)], ref.at[pl.ds(slot * pitch + ROWS, ROWS)],
            ssem.at[slot], rsem.at[slot], twin,
        )

    def arrive(*keys):
        for key in keys:
            got[key].wait_recv()

    def to_ring_first(names):
        for name in names:
            hop(name, "0a", "2a", UP)
            hop(name, "0b", "1b", DOWN)
        for name in names:
            hop(name, "0b", "2b", UP)
            hop(name, "0a", "1a", DOWN)

    def to_side_first(names):
        for name in names:
            hop(name, "0", "3", SIDE)
        across(names[1], 0)

    to_ring_first(("ti", "tt"))
    to_side_first(("ti", "tt"))
    for copy in loads[2:]:
        copy.wait()
    si[0:ROWS] = unit_of(img_raw[...])[0].astype(jnp.bfloat16)
    st[0:ROWS] = unit_of(txt_raw[...])[0].astype(jnp.bfloat16)
    to_side_first(("si", "st"))

    def clear(i, _):
        rows = pl.ds(pl.multiple_of(i * ROWS, ROWS), ROWS)
        iacc[rows, :] = jnp.zeros((ROWS, iacc.shape[1]), jnp.float32)
        tacc[pl.ds(pl.multiple_of(i * 2 * ROWS, 2 * ROWS), 2 * ROWS), :] = jnp.zeros(
            (2 * ROWS, tacc.shape[1]), jnp.float32
        )
        return 0

    lax.fori_loop(0, 8, clear, 0)

    def teacher_value(zt):
        return 0.5 - 0.5 * jnp.tanh(half_scale * zt + half_bias)

    WIDE = 4 * ROWS

    def columns(pair):
        return pl.ds(pl.multiple_of(pair * WIDE, WIDE), WIDE)

    def teach(first, count, pair):
        return teacher_value(dot(ti[first : first + count], tt[columns(pair), :], NT))

    def learn(first, count, pair, teacher, diagonal=False):
        rows = slice(first, first + count)
        cols = columns(pair)
        value = jnp.tanh(half_scale * dot(si[rows], st[cols, :], NT) + half_bias) + teacher
        if diagonal:
            row = lax.broadcasted_iota(jnp.int32, (ROWS, WIDE), 0)
            col = lax.broadcasted_iota(jnp.int32, (ROWS, WIDE), 1)
            positive = jnp.where(row == col, 1.0, 0.0)
            gs[0:ROWS] = (value[:ROWS] - positive).astype(jnp.bfloat16)
            gs[ROWS:count] = value[ROWS:].astype(jnp.bfloat16)
        else:
            gs[0:count] = value.astype(jnp.bfloat16)
        g = gs[0:count]
        iacc[rows] += dot(g, st[cols, :], NN)
        tacc[cols, :] += dot(g, si[rows], TN)

    def over(begin, end, one):
        lax.fori_loop(begin, end, lambda pair, _: (one(pair), 0)[1], 0)

    def relay(names):
        arrive(*[(name, part) for part in ("2a", "1b") for name in names])
        for name in names:
            hop(name, "2a", "4a", UP)
            hop(name, "1b", "4b", DOWN)

    def to_ring(names):
        for name in names:
            hop(name, "3", "6", UP)
            hop(name, "3", "5", DOWN)

    def near_across(name, chips):
        for chip in chips:
            arrive((name, {"3": "3", "1": "1a", "2": "2b"}[chip]))
            across(name, slot_of[chip])

    def far_to_side(names):
        arrive(*[(name, part) for part in ("4a", "4b") for name in names])
        for name in names:
            hop(name, "4", "7", SIDE)
        across(names[1], slot_of["4"])

    def late_across(name, chips):
        for chip in chips:
            arrive((name, chip))
            across(name, slot_of[chip])

    TEACHER, STUDENT = ("ti", "tt"), ("si", "st")
    relay(TEACHER)
    to_ring_first(STUDENT)
    near_across("tt", "312")
    far_to_side(TEACHER)
    arrive(*[("ti", part) for part in ("3", "1a", "2b")])
    arrive(*[("ttc", slot) for slot in range(4)])

    def teach_first(pair):
        pa1[pair] = teach(0, 512, pair)

    over(0, 2, teach_first)
    near_across("st", "3")
    relay(STUDENT)
    arrive(("si", "3"))
    to_ring(TEACHER)
    to_ring(STUDENT)
    arrive(("stc", 0), ("stc", 1))
    learn(0, 256, 0, pa1[0, 0:256], True)
    near_across("st", "12")
    arrive(("si", "1a"), ("si", "2b"))
    learn(256, 256, 0, pa1[0, 256:512])
    far_to_side(STUDENT)
    arrive(("stc", 2), ("stc", 3))
    learn(0, 512, 1, pa1[1])

    late_across("tt", "7")
    arrive(("ti", "7"))

    def teach_new2(pair):
        pn2[pair] = teach(512, 256, pair)

    over(0, 2, teach_new2)
    arrive(("ttc", 4), ("ttc", 5))
    pa2[...] = teach(0, 768, 2)

    late_across("st", "7")
    arrive(("si", "7"))
    over(0, 2, lambda pair: learn(512, 256, pair, pn2[pair]))
    arrive(("stc", 4), ("stc", 5))
    learn(0, 768, 2, pa2[...])

    late_across("tt", "56")
    arrive(("ti", "5"), ("ti", "6"))

    def teach_new3(pair):
        pn3[pair] = teach(768, 256, pair)

    over(0, 3, teach_new3)
    arrive(("ttc", 6), ("ttc", 7))
    pa3[...] = teach(0, 1024, 3)

    late_across("st", "56")
    arrive(("si", "5"), ("si", "6"))
    def give(slots):
        for p in slots:
            lo = p * 2 * ROWS + ROWS
            tb[p * ROWS : (p + 1) * ROWS] = tacc[lo : lo + ROWS].astype(jnp.bfloat16)
        for p in slots:
            rows = pl.ds(p * ROWS, ROWS)
            got["g", p] = remote(tb.at[rows], crecv.at[rows], csend_g.at[p], crecv_g.at[p], twin)

    def img_part(chip):
        slot = slot_of[chip]
        return iacc[slot * ROWS : (slot + 1) * ROWS]

    def txt_part(chip):
        slot = slot_of[chip]
        mine = tacc[slot * 2 * ROWS : slot * 2 * ROWS + ROWS]
        return mine + crecv[slot * ROWS : (slot + 1) * ROWS].astype(jnp.float32)

    part = {"i": img_part, "t": txt_part}
    out_buf = {"i": ib, "t": ts}
    in_buf = {"i": irecv, "t": trecv}
    out_sem = {"i": isend, "t": tsend}
    in_sem = {"i": irsem, "t": trsem}
    peers = {"i": img_devs, "t": txt_devs}
    piece = {"1": (0, ROWS, 0), "2": (ROWS, ROWS, 1), "3": (2 * ROWS, ROWS, 2), "4": (3 * ROWS, ROWS, 3),
             "5": (4 * ROWS, ROWS, 4), "6": (5 * ROWS, ROWS, 5), "7": (6 * ROWS, ROWS, 6)}
    for chip, first_sem in (("1", 0), ("2", 1), ("4", 3)):
        row = piece[chip][0]
        piece[chip + "a"] = (row, HALF, first_sem)
        piece[chip + "b"] = (row + HALF, HALF, first_sem + 7 if chip != "4" else 9)

    def rows_of(ref, key):
        row, count, _ = piece[key]
        return ref[row : row + count]

    def fill(stream, key, value):
        row, count, _ = piece[key]
        out_buf[stream][row : row + count] = value.astype(jnp.bfloat16)

    def put(stream, key, way):
        row, count, sem = piece[key]
        rows = pl.ds(row, count)
        got[stream, "sum" + key] = remote(
            out_buf[stream].at[rows], in_buf[stream].at[rows],
            out_sem[stream].at[sem], in_sem[stream].at[sem], peers[stream][way],
        )

    def came(stream, key):
        arrive((stream, "sum" + key))
        return rows_of(in_buf[stream], key).astype(jnp.float32)

    def send_7(stream):
        fill(stream, "7", part[stream]("7"))
        put(stream, "7", SIDE)

    def send_near(stream):
        fill(stream, "1", part[stream]("1"))
        fill(stream, "2", part[stream]("2"))
        put(stream, "1a", UP)
        put(stream, "2b", DOWN)

    def send_56(stream):
        fill(stream, "5", part[stream]("5"))
        fill(stream, "6", part[stream]("6"))
        put(stream, "5", UP)
        put(stream, "6", DOWN)

    def send_far(stream):
        fill(stream, "4", part[stream]("4") + came(stream, "7"))
        put(stream, "4b", UP)
        put(stream, "4a", DOWN)

    def send_side(stream):
        fill(stream, "3", part[stream]("3") + came(stream, "5") + came(stream, "6"))
        put(stream, "3", SIDE)

    def send_rest(stream):
        fill(stream, "1b", part[stream]("1")[HALF:] + came(stream, "4b"))
        fill(stream, "2a", part[stream]("2")[:HALF] + came(stream, "4a"))
        put(stream, "1b", UP)
        put(stream, "2a", DOWN)

    def total(stream):
        for key in ("1a", "1b", "2a", "2b"):
            arrive((stream, "sum" + key))
        near = rows_of(in_buf[stream], "1").astype(jnp.float32) + rows_of(in_buf[stream], "2").astype(jnp.float32)
        return logit_scale * (part[stream]("0") + near + came(stream, "3"))

    learn(768, 256, 1, pn3[1])
    give((2, 3))
    learn(768, 256, 2, pn3[2])
    give((5, 4))
    arrive(("stc", 6), ("stc", 7))
    learn(256, 256, 3, pa3[256:512])
    send_near("i")
    arrive(("g", 2), ("g", 3))
    send_near("t")
    learn(512, 256, 3, pa3[512:768])
    send_7("i")
    arrive(("g", 5))
    send_7("t")
    learn(0, 256, 3, pa3[0:256])
    learn(768, 256, 3, pa3[768:1024])
    give((6, 7))
    learn(768, 256, 0, pn3[0])
    give((1, 0))
    send_56("i")
    arrive(("g", 6), ("g", 7))
    send_56("t")
    arrive(("g", 4))
    send_far("i")
    send_far("t")
    arrive(("g", 1))
    send_side("i")
    send_side("t")
    send_rest("i")
    send_rest("t")
    grads[0:ROWS] = back(total("i"), img_raw[...])
    arrive(("g", 0))
    grads[ROWS : 2 * ROWS] = back(total("t"), txt_raw[...])

    for copy in sent:
        copy.wait_send()


def body(student_img, student_txt, teacher_img, teacher_txt):
    width = student_img.shape[1]
    t_width = teacher_img.shape[1]
    bf16, f32 = jnp.bfloat16, jnp.float32
    vmem = pl.BlockSpec(memory_space=pltpu.VMEM)
    dma = pltpu.SemaphoreType.DMA((10,))
    both = pl.pallas_call(
        kernel,
        out_shape=jax.ShapeDtypeStruct((2 * ROWS, width), f32),
        in_specs=[pl.BlockSpec(memory_space=pl.ANY)] * 4,
        out_specs=vmem,
        scratch_shapes=[
            pltpu.VMEM((ROWS, width), bf16),
            pltpu.VMEM((ROWS, width), bf16),
            pltpu.VMEM((ROWS, t_width), bf16),
            pltpu.VMEM((ROWS, t_width), bf16),
            pltpu.VMEM((8 * ROWS, width), bf16),
            pltpu.VMEM((8 * ROWS, t_width), bf16),
            pltpu.VMEM((16 * ROWS, width), bf16),
            pltpu.VMEM((16 * ROWS, t_width), bf16),
            pltpu.VMEM((2, 4 * ROWS, 4 * ROWS), f32),
            pltpu.VMEM((2, 2 * ROWS, 4 * ROWS), f32),
            pltpu.VMEM((6 * ROWS, 4 * ROWS), f32),
            pltpu.VMEM((3, 2 * ROWS, 4 * ROWS), f32),
            pltpu.VMEM((8 * ROWS, 4 * ROWS), f32),
            pltpu.VMEM((8 * ROWS, 4 * ROWS), bf16),
            pltpu.VMEM((8 * ROWS, width), f32),
            pltpu.VMEM((16 * ROWS, width), f32),
            pltpu.VMEM((8 * ROWS, width), bf16),
            pltpu.VMEM((8 * ROWS, width), bf16),
            pltpu.VMEM((8 * ROWS, width), bf16),
            pltpu.VMEM((8 * ROWS, width), bf16),
            pltpu.VMEM((7 * ROWS, width), bf16),
            pltpu.VMEM((7 * ROWS, width), bf16),
        ]
        + [dma] * 19,
        compiler_params=pltpu.CompilerParams(
            collective_id=0, has_side_effects=True, vmem_limit_bytes=62 << 20
        ),
    )(student_img, student_txt, teacher_img, teacher_txt)
    return both[:ROWS], both[ROWS:]


def solution(mesh):
    rows = P(("blk", "narrow"), None)
    return jax.shard_map(body, mesh=mesh, in_specs=(rows,) * 4, out_specs=(rows, rows), check_vma=False)
```

```python
import jax
import jax.numpy as jnp
from jax import lax
from jax.experimental import pallas as pl
from jax.experimental.pallas import tpu as pltpu
from jax.sharding import PartitionSpec as P

epsilon = 1e-06
logit_scale = 100.0
logit_bias = -4.0
half_scale = 0.5 * logit_scale
half_bias = 0.5 * logit_bias

ROWS = 128
MESH_ID = pl.DeviceIdType.MESH
NT = (((1,), (1,)), ((), ()))
NN = (((1,), (0,)), ((), ()))
TN = (((0,), (0,)), ((), ()))

HALF = ROWS // 2


def dot(a, b, dims):
    return lax.dot_general(a, b, dims, preferred_element_type=jnp.float32)


def unit_of(raw):
    x = raw.astype(jnp.float32)
    radius = jnp.sqrt(jnp.sum(x * x, axis=1, keepdims=True) + epsilon)
    return x / radius, radius


def back(grad, raw):
    unit, radius = unit_of(raw)
    along = jnp.sum(unit * grad, axis=1, keepdims=True)
    return (grad - unit * along) / radius


def kernel(
    img_hbm, txt_hbm, timg_hbm, ttxt_hbm, grads, img_raw, txt_raw, timg_raw, ttxt_raw,
    si, ti, st, tt, pa1, pn2, pa2, pn3, pa3, gs, iacc, tacc, ib, tb, ts, crecv, irecv, trecv,
    send_si, send_ti, send_st, send_tt, recv_si, recv_ti, recv_st, recv_tt,
    csend_st, csend_tt, crecv_st, crecv_tt, csend_g, crecv_g, load, isend, irsem, tsend, trsem,
):
    b = lax.axis_index("blk")
    n = lax.axis_index("narrow")
    core = lax.rem(b, 2)
    z = b // 4
    x = 2 * lax.rem(b // 2, 2) + n // 4
    y = lax.rem(n, 4)
    odd = lax.rem(x, 2)

    def device(x, y, z, core):
        return ((z * 2 + x // 2) * 2 + core, lax.rem(x, 2) * 4 + y)

    def step(v, by):
        return lax.rem(v + 4 + by, 4)

    x_img = x + 1 - 2 * odd
    x_txt = lax.rem(x + 3 + 2 * odd, 4)
    img_up = device(x, step(y, 1), z, core)
    img_down = device(x, step(y, -1), z, core)
    img_side = device(x_img, y, z, core)
    txt_up = device(x, y, step(z, 1), core)
    txt_down = device(x, y, step(z, -1), core)
    txt_side = device(x_txt, y, z, core)
    twin = device(x, y, z, 1 - core)

    barrier = pltpu.get_barrier_semaphore()
    for peer in (img_up, img_down, img_side, txt_up, txt_down, txt_side, twin):
        pl.semaphore_signal(barrier, inc=1, device_id=peer, device_id_type=MESH_ID)

    loads = [
        pltpu.make_async_copy(src, dst, load.at[i])
        for i, (src, dst) in enumerate(
            ((timg_hbm, timg_raw), (ttxt_hbm, ttxt_raw), (img_hbm, img_raw), (txt_hbm, txt_raw))
        )
    ]
    for copy in loads:
        copy.start()
    for copy in loads[:2]:
        copy.wait()
    ti[0:ROWS] = unit_of(timg_raw[...])[0].astype(jnp.bfloat16)
    tt[0:ROWS] = unit_of(ttxt_raw[...])[0].astype(jnp.bfloat16)

    pl.semaphore_wait(barrier, 7)

    sent = []

    def remote(src, dst, ssem, rsem, dev):
        copy = pltpu.make_async_remote_copy(
            src_ref=src, dst_ref=dst, send_sem=ssem, recv_sem=rsem, device_id=dev, device_id_type=MESH_ID
        )
        copy.start()
        sent.append(copy)
        return copy

    img_devs = (img_up, img_down, img_side)
    txt_devs = (txt_up, txt_down, txt_side)
    arrays = {
        "ti": (ti, send_ti, recv_ti, ROWS, img_devs),
        "si": (si, send_si, recv_si, ROWS, img_devs),
        "tt": (tt, send_tt, recv_tt, 2 * ROWS, txt_devs),
        "st": (st, send_st, recv_st, 2 * ROWS, txt_devs),
    }
    got = {}
    UP, DOWN, SIDE = 0, 1, 2
    slot_of = {"0": 0, "3": 1, "1": 2, "2": 3, "4": 4, "7": 5, "5": 6, "6": 7}
    places = {}
    for chip, slot in slot_of.items():
        places[chip] = (slot, 0, ROWS)
        places[chip + "a"] = (slot, 0, HALF)
        places[chip + "b"] = (slot, HALF, HALF)
    index = {k: i for i, k in enumerate(("1a", "1b", "2a", "2b", "3", "4a", "4b", "7", "5", "6"))}

    def hop(name, src, dst, way):
        ref, ssem, rsem, pitch, devs = arrays[name]
        s_slot, s_row, count = places[src]
        d_slot, d_row, _ = places[dst]
        got[name, dst] = remote(
            ref.at[pl.ds(s_slot * pitch + s_row, count)], ref.at[pl.ds(d_slot * pitch + d_row, count)],
            ssem.at[index[dst]], rsem.at[index[dst]], devs[way],
        )

    def across(name, slot):
        ref, _, _, pitch, _ = arrays[name]
        ssem, rsem = (csend_tt, crecv_tt) if name == "tt" else (csend_st, crecv_st)
        got[name + "c", slot] = remote(
            ref.at[pl.ds(slot * pitch, ROWS)], ref.at[pl.ds(slot * pitch + ROWS, ROWS)],
            ssem.at[slot], rsem.at[slot], twin,
        )

    def arrive(*keys):
        for key in keys:
            got[key].wait_recv()

    def to_ring_first(names):
        for name in names:
            hop(name, "0a", "2a", UP)
            hop(name, "0b", "1b", DOWN)
        for name in names:
            hop(name, "0b", "2b", UP)
            hop(name, "0a", "1a", DOWN)

    def to_side_first(names):
        for name in names:
            hop(name, "0", "3", SIDE)
        across(names[1], 0)

    to_ring_first(("ti", "tt"))
    to_side_first(("ti", "tt"))
    for copy in loads[2:]:
        copy.wait()
    si[0:ROWS] = unit_of(img_raw[...])[0].astype(jnp.bfloat16)
    st[0:ROWS] = unit_of(txt_raw[...])[0].astype(jnp.bfloat16)
    to_side_first(("si", "st"))

    def clear(i, _):
        rows = pl.ds(pl.multiple_of(i * ROWS, ROWS), ROWS)
        iacc[rows, :] = jnp.zeros((ROWS, iacc.shape[1]), jnp.float32)
        tacc[pl.ds(pl.multiple_of(i * 2 * ROWS, 2 * ROWS), 2 * ROWS), :] = jnp.zeros(
            (2 * ROWS, tacc.shape[1]), jnp.float32
        )
        return 0

    lax.fori_loop(0, 8, clear, 0)

    def teacher_value(zt):
        return 0.5 - 0.5 * jnp.tanh(half_scale * zt + half_bias)

    WIDE = 4 * ROWS

    def columns(pair):
        return pl.ds(pl.multiple_of(pair * WIDE, WIDE), WIDE)

    def teach(first, count, pair):
        return teacher_value(dot(ti[first : first + count], tt[columns(pair), :], NT))

    def learn(first, count, pair, teacher, diagonal=False):
        rows = slice(first, first + count)
        cols = columns(pair)
        value = jnp.tanh(half_scale * dot(si[rows], st[cols, :], NT) + half_bias) + teacher
        if diagonal:
            row = lax.broadcasted_iota(jnp.int32, (ROWS, WIDE), 0)
            col = lax.broadcasted_iota(jnp.int32, (ROWS, WIDE), 1)
            positive = jnp.where(row == col, 1.0, 0.0)
            gs[0:ROWS] = (value[:ROWS] - positive).astype(jnp.bfloat16)
            gs[ROWS:count] = value[ROWS:].astype(jnp.bfloat16)
        else:
            gs[0:count] = value.astype(jnp.bfloat16)
        g = gs[0:count]
        iacc[rows] += dot(g, st[cols, :], NN)
        tacc[cols, :] += dot(g, si[rows], TN)

    def over(begin, end, one):
        lax.fori_loop(begin, end, lambda pair, _: (one(pair), 0)[1], 0)

    def relay(names):
        arrive(*[(name, part) for part in ("2a", "1b") for name in names])
        for name in names:
            hop(name, "2a", "4a", UP)
            hop(name, "1b", "4b", DOWN)

    def to_ring(names):
        for name in names:
            hop(name, "3", "6", UP)
            hop(name, "3", "5", DOWN)

    def near_across(name, chips):
        for chip in chips:
            arrive((name, {"3": "3", "1": "1a", "2": "2b"}[chip]))
            across(name, slot_of[chip])

    def far_to_side(names):
        arrive(*[(name, part) for part in ("4a", "4b") for name in names])
        for name in names:
            hop(name, "4", "7", SIDE)
        across(names[1], slot_of["4"])

    def late_across(name, chips):
        for chip in chips:
            arrive((name, chip))
            across(name, slot_of[chip])

    TEACHER, STUDENT = ("ti", "tt"), ("si", "st")
    relay(TEACHER)
    to_ring_first(STUDENT)
    near_across("tt", "312")
    far_to_side(TEACHER)
    arrive(*[("ti", part) for part in ("3", "1a", "2b")])
    arrive(*[("ttc", slot) for slot in range(4)])

    def teach_first(pair):
        pa1[pair] = teach(0, 512, pair)

    over(0, 2, teach_first)
    near_across("st", "3")
    relay(STUDENT)
    arrive(("si", "3"))
    to_ring(TEACHER)
    to_ring(STUDENT)
    arrive(("stc", 0), ("stc", 1))
    learn(0, 256, 0, pa1[0, 0:256], True)
    near_across("st", "12")
    arrive(("si", "1a"), ("si", "2b"))
    learn(256, 256, 0, pa1[0, 256:512])
    far_to_side(STUDENT)
    arrive(("stc", 2), ("stc", 3))
    learn(0, 512, 1, pa1[1])

    late_across("tt", "7")
    arrive(("ti", "7"))

    def teach_new2(pair):
        pn2[pair] = teach(512, 256, pair)

    over(0, 2, teach_new2)
    arrive(("ttc", 4), ("ttc", 5))
    pa2[...] = teach(0, 768, 2)

    late_across("st", "7")
    arrive(("si", "7"))
    over(0, 2, lambda pair: learn(512, 256, pair, pn2[pair]))
    arrive(("stc", 4), ("stc", 5))
    learn(0, 768, 2, pa2[...])

    late_across("tt", "56")
    arrive(("ti", "5"), ("ti", "6"))

    def teach_new3(pair):
        pn3[pair] = teach(768, 256, pair)

    over(0, 3, teach_new3)
    arrive(("ttc", 6), ("ttc", 7))
    pa3[...] = teach(0, 1024, 3)

    late_across("st", "56")
    arrive(("si", "5"), ("si", "6"))
    def give(slots):
        for p in slots:
            lo = p * 2 * ROWS + ROWS
            tb[p * ROWS : (p + 1) * ROWS] = tacc[lo : lo + ROWS].astype(jnp.bfloat16)
        for p in slots:
            rows = pl.ds(p * ROWS, ROWS)
            got["g", p] = remote(tb.at[rows], crecv.at[rows], csend_g.at[p], crecv_g.at[p], twin)

    def img_part(chip):
        slot = slot_of[chip]
        return iacc[slot * ROWS : (slot + 1) * ROWS]

    def txt_part(chip):
        slot = slot_of[chip]
        mine = tacc[slot * 2 * ROWS : slot * 2 * ROWS + ROWS]
        return mine + crecv[slot * ROWS : (slot + 1) * ROWS].astype(jnp.float32)

    part = {"i": img_part, "t": txt_part}
    out_buf = {"i": ib, "t": ts}
    in_buf = {"i": irecv, "t": trecv}
    out_sem = {"i": isend, "t": tsend}
    in_sem = {"i": irsem, "t": trsem}
    peers = {"i": img_devs, "t": txt_devs}
    piece = {"1": (0, ROWS, 0), "2": (ROWS, ROWS, 1), "3": (2 * ROWS, ROWS, 2), "4": (3 * ROWS, ROWS, 3),
             "5": (4 * ROWS, ROWS, 4), "6": (5 * ROWS, ROWS, 5), "7": (6 * ROWS, ROWS, 6)}
    QUARTER = ROWS // 4
    piece["1a"] = (0, HALF, 0)
    piece["2b"] = (ROWS + HALF, HALF, 1)
    for i, (chip, half) in enumerate((("1", "b"), ("2", "a"), ("4", "a"), ("4", "b"))):
        row = piece[chip][0] + (HALF if half == "b" else 0)
        for q in (0, 1):
            piece[chip + half + str(q)] = (row + q * QUARTER, QUARTER, 7 + 2 * i + q)

    def rows_of(ref, key):
        row, count, _ = piece[key]
        return ref[row : row + count]

    def fill(stream, key, value):
        row, count, _ = piece[key]
        out_buf[stream][row : row + count] = value.astype(jnp.bfloat16)

    def put(stream, key, way):
        row, count, sem = piece[key]
        rows = pl.ds(row, count)
        got[stream, "sum" + key] = remote(
            out_buf[stream].at[rows], in_buf[stream].at[rows],
            out_sem[stream].at[sem], in_sem[stream].at[sem], peers[stream][way],
        )

    def came(stream, key):
        arrive((stream, "sum" + key))
        return rows_of(in_buf[stream], key).astype(jnp.float32)

    def send_7(stream):
        fill(stream, "7", part[stream]("7"))
        put(stream, "7", SIDE)

    def send_near(stream):
        fill(stream, "1", part[stream]("1"))
        fill(stream, "2", part[stream]("2"))
        put(stream, "1a", UP)
        put(stream, "2b", DOWN)

    def send_56(stream):
        fill(stream, "5", part[stream]("5"))
        fill(stream, "6", part[stream]("6"))
        put(stream, "5", UP)
        put(stream, "6", DOWN)

    def send_far(stream):
        fill(stream, "4", part[stream]("4") + came(stream, "7"))
        for q in "01":
            put(stream, "4b" + q, UP)
            put(stream, "4a" + q, DOWN)

    def send_side(stream):
        fill(stream, "3", part[stream]("3") + came(stream, "5") + came(stream, "6"))
        put(stream, "3", SIDE)

    def send_rest(stream, q):
        low, high = q * QUARTER, (q + 1) * QUARTER
        one, two, q = part[stream]("1"), part[stream]("2"), str(q)
        fill(stream, "1b" + q, one[HALF + low : HALF + high] + came(stream, "4b" + q))
        put(stream, "1b" + q, UP)
        fill(stream, "2a" + q, two[low:high] + came(stream, "4a" + q))
        put(stream, "2a" + q, DOWN)

    def total(stream):
        for key in ("1a", "1b0", "1b1", "2a0", "2a1", "2b"):
            arrive((stream, "sum" + key))
        near = rows_of(in_buf[stream], "1").astype(jnp.float32) + rows_of(in_buf[stream], "2").astype(jnp.float32)
        return logit_scale * (part[stream]("0") + near + came(stream, "3"))

    learn(768, 256, 1, pn3[1])
    give((2, 3))
    learn(768, 256, 2, pn3[2])
    give((5, 4))
    arrive(("stc", 6), ("stc", 7))
    learn(256, 256, 3, pa3[256:512])
    send_near("i")
    arrive(("g", 2), ("g", 3))
    send_near("t")
    learn(512, 256, 3, pa3[512:768])
    send_7("i")
    arrive(("g", 5))
    send_7("t")
    learn(0, 256, 3, pa3[0:256])
    learn(768, 256, 3, pa3[768:1024])
    give((6, 7))
    learn(768, 256, 0, pn3[0])
    give((1, 0))
    send_56("i")
    arrive(("g", 6), ("g", 7))
    send_56("t")
    arrive(("g", 4))
    send_far("i")
    send_far("t")
    arrive(("g", 1))
    send_side("i")
    send_side("t")
    for q in (0, 1):
        send_rest("i", q)
        send_rest("t", q)
    grads[0:ROWS] = back(total("i"), img_raw[...])
    arrive(("g", 0))
    grads[ROWS : 2 * ROWS] = back(total("t"), txt_raw[...])

    for copy in sent:
        copy.wait_send()


def body(student_img, student_txt, teacher_img, teacher_txt):
    width = student_img.shape[1]
    t_width = teacher_img.shape[1]
    bf16, f32 = jnp.bfloat16, jnp.float32
    vmem = pl.BlockSpec(memory_space=pltpu.VMEM)
    dma = pltpu.SemaphoreType.DMA((15,))
    both = pl.pallas_call(
        kernel,
        out_shape=jax.ShapeDtypeStruct((2 * ROWS, width), f32),
        in_specs=[pl.BlockSpec(memory_space=pl.ANY)] * 4,
        out_specs=vmem,
        scratch_shapes=[
            pltpu.VMEM((ROWS, width), bf16),
            pltpu.VMEM((ROWS, width), bf16),
            pltpu.VMEM((ROWS, t_width), bf16),
            pltpu.VMEM((ROWS, t_width), bf16),
            pltpu.VMEM((8 * ROWS, width), bf16),
            pltpu.VMEM((8 * ROWS, t_width), bf16),
            pltpu.VMEM((16 * ROWS, width), bf16),
            pltpu.VMEM((16 * ROWS, t_width), bf16),
            pltpu.VMEM((2, 4 * ROWS, 4 * ROWS), f32),
            pltpu.VMEM((2, 2 * ROWS, 4 * ROWS), f32),
            pltpu.VMEM((6 * ROWS, 4 * ROWS), f32),
            pltpu.VMEM((3, 2 * ROWS, 4 * ROWS), f32),
            pltpu.VMEM((8 * ROWS, 4 * ROWS), f32),
            pltpu.VMEM((8 * ROWS, 4 * ROWS), bf16),
            pltpu.VMEM((8 * ROWS, width), f32),
            pltpu.VMEM((16 * ROWS, width), f32),
            pltpu.VMEM((8 * ROWS, width), bf16),
            pltpu.VMEM((8 * ROWS, width), bf16),
            pltpu.VMEM((8 * ROWS, width), bf16),
            pltpu.VMEM((8 * ROWS, width), bf16),
            pltpu.VMEM((7 * ROWS, width), bf16),
            pltpu.VMEM((7 * ROWS, width), bf16),
        ]
        + [dma] * 19,
        compiler_params=pltpu.CompilerParams(
            collective_id=0, has_side_effects=True, vmem_limit_bytes=62 << 20
        ),
    )(student_img, student_txt, teacher_img, teacher_txt)
    return both[:ROWS], both[ROWS:]


def solution(mesh):
    rows = P(("blk", "narrow"), None)
    return jax.shard_map(body, mesh=mesh, in_specs=(rows,) * 4, out_specs=(rows, rows), check_vma=False)
```

```python
import jax
import jax.numpy as jnp
from jax import lax
from jax.experimental import pallas as pl
from jax.experimental.pallas import tpu as pltpu
from jax.sharding import PartitionSpec as P

epsilon = 1e-06
logit_scale = 100.0
logit_bias = -4.0
half_scale = 0.5 * logit_scale
half_bias = 0.5 * logit_bias

ROWS = 128
MESH_ID = pl.DeviceIdType.MESH
NT = (((1,), (1,)), ((), ()))
NN = (((1,), (0,)), ((), ()))
TN = (((0,), (0,)), ((), ()))

HALF = ROWS // 2


def dot(a, b, dims):
    return lax.dot_general(a, b, dims, preferred_element_type=jnp.float32)


def unit_of(raw):
    x = raw.astype(jnp.float32)
    radius = jnp.sqrt(jnp.sum(x * x, axis=1, keepdims=True) + epsilon)
    return x / radius, radius


def back(grad, raw):
    unit, radius = unit_of(raw)
    along = jnp.sum(unit * grad, axis=1, keepdims=True)
    return (grad - unit * along) / radius


def kernel(
    img_hbm, txt_hbm, timg_hbm, ttxt_hbm, grads, img_raw, txt_raw, timg_raw, ttxt_raw,
    si, ti, st, tt, pa1, pn2, pa2, pn3, pa3, gs, iacc, tacc, ib, tb, ts, crecv, irecv, trecv,
    send_si, send_ti, send_st, send_tt, recv_si, recv_ti, recv_st, recv_tt,
    csend_st, csend_tt, crecv_st, crecv_tt, csend_g, crecv_g, load, isend, irsem, tsend, trsem,
):
    b = lax.axis_index("blk")
    n = lax.axis_index("narrow")
    core = lax.rem(b, 2)
    z = b // 4
    x = 2 * lax.rem(b // 2, 2) + n // 4
    y = lax.rem(n, 4)
    odd = lax.rem(x, 2)

    def device(x, y, z, core):
        return ((z * 2 + x // 2) * 2 + core, lax.rem(x, 2) * 4 + y)

    def step(v, by):
        return lax.rem(v + 4 + by, 4)

    x_img = x + 1 - 2 * odd
    x_txt = lax.rem(x + 3 + 2 * odd, 4)
    img_up = device(x, step(y, 1), z, core)
    img_down = device(x, step(y, -1), z, core)
    img_side = device(x_img, y, z, core)
    txt_up = device(x, y, step(z, 1), core)
    txt_down = device(x, y, step(z, -1), core)
    txt_side = device(x_txt, y, z, core)
    twin = device(x, y, z, 1 - core)

    barrier = pltpu.get_barrier_semaphore()
    for peer in (img_up, img_down, img_side, txt_up, txt_down, txt_side, twin):
        pl.semaphore_signal(barrier, inc=1, device_id=peer, device_id_type=MESH_ID)

    loads = [
        pltpu.make_async_copy(src, dst, load.at[i])
        for i, (src, dst) in enumerate(
            ((timg_hbm, timg_raw), (ttxt_hbm, ttxt_raw), (img_hbm, img_raw), (txt_hbm, txt_raw))
        )
    ]
    for copy in loads:
        copy.start()
    for copy in loads[:2]:
        copy.wait()
    ti[0:ROWS] = unit_of(timg_raw[...])[0].astype(jnp.bfloat16)
    tt[0:ROWS] = unit_of(ttxt_raw[...])[0].astype(jnp.bfloat16)

    pl.semaphore_wait(barrier, 7)

    sent = []

    def remote(src, dst, ssem, rsem, dev):
        copy = pltpu.make_async_remote_copy(
            src_ref=src, dst_ref=dst, send_sem=ssem, recv_sem=rsem, device_id=dev, device_id_type=MESH_ID
        )
        copy.start()
        sent.append(copy)
        return copy

    img_devs = (img_up, img_down, img_side)
    txt_devs = (txt_up, txt_down, txt_side)
    arrays = {
        "ti": (ti, send_ti, recv_ti, ROWS, img_devs),
        "si": (si, send_si, recv_si, ROWS, img_devs),
        "tt": (tt, send_tt, recv_tt, 2 * ROWS, txt_devs),
        "st": (st, send_st, recv_st, 2 * ROWS, txt_devs),
    }
    got = {}
    UP, DOWN, SIDE = 0, 1, 2
    slot_of = {"0": 0, "3": 1, "1": 2, "2": 3, "4": 4, "7": 5, "5": 6, "6": 7}
    places = {}
    for chip, slot in slot_of.items():
        places[chip] = (slot, 0, ROWS)
        places[chip + "a"] = (slot, 0, HALF)
        places[chip + "b"] = (slot, HALF, HALF)
    index = {k: i for i, k in enumerate(("1a", "1b", "2a", "2b", "3", "4a", "4b", "7", "5", "6"))}

    def hop(name, src, dst, way):
        ref, ssem, rsem, pitch, devs = arrays[name]
        s_slot, s_row, count = places[src]
        d_slot, d_row, _ = places[dst]
        got[name, dst] = remote(
            ref.at[pl.ds(s_slot * pitch + s_row, count)], ref.at[pl.ds(d_slot * pitch + d_row, count)],
            ssem.at[index[dst]], rsem.at[index[dst]], devs[way],
        )

    def across(name, slot):
        ref, _, _, pitch, _ = arrays[name]
        ssem, rsem = (csend_tt, crecv_tt) if name == "tt" else (csend_st, crecv_st)
        got[name + "c", slot] = remote(
            ref.at[pl.ds(slot * pitch, ROWS)], ref.at[pl.ds(slot * pitch + ROWS, ROWS)],
            ssem.at[slot], rsem.at[slot], twin,
        )

    def arrive(*keys):
        for key in keys:
            got[key].wait_recv()

    def to_ring_first(names):
        for name in names:
            hop(name, "0a", "2a", UP)
            hop(name, "0b", "1b", DOWN)
        for name in names:
            hop(name, "0b", "2b", UP)
            hop(name, "0a", "1a", DOWN)

    def to_side_first(names):
        for name in names:
            hop(name, "0", "3", SIDE)
        across(names[1], 0)

    to_ring_first(("ti", "tt"))
    to_side_first(("ti", "tt"))
    for copy in loads[2:]:
        copy.wait()
    si[0:ROWS] = unit_of(img_raw[...])[0].astype(jnp.bfloat16)
    st[0:ROWS] = unit_of(txt_raw[...])[0].astype(jnp.bfloat16)
    to_side_first(("si", "st"))

    def clear(i, _):
        rows = pl.ds(pl.multiple_of(i * ROWS, ROWS), ROWS)
        iacc[rows, :] = jnp.zeros((ROWS, iacc.shape[1]), jnp.float32)
        tacc[pl.ds(pl.multiple_of(i * 2 * ROWS, 2 * ROWS), 2 * ROWS), :] = jnp.zeros(
            (2 * ROWS, tacc.shape[1]), jnp.float32
        )
        return 0

    lax.fori_loop(0, 8, clear, 0)

    def teacher_value(zt):
        return 0.5 - 0.5 * jnp.tanh(half_scale * zt + half_bias)

    WIDE = 4 * ROWS

    def columns(pair):
        return pl.ds(pl.multiple_of(pair * WIDE, WIDE), WIDE)

    def teach(first, count, pair):
        return teacher_value(dot(ti[first : first + count], tt[columns(pair), :], NT))

    def learn(first, count, pair, teacher, diagonal=False):
        rows = slice(first, first + count)
        cols = columns(pair)
        value = jnp.tanh(half_scale * dot(si[rows], st[cols, :], NT) + half_bias) + teacher
        if diagonal:
            row = lax.broadcasted_iota(jnp.int32, (ROWS, WIDE), 0)
            col = lax.broadcasted_iota(jnp.int32, (ROWS, WIDE), 1)
            positive = jnp.where(row == col, 1.0, 0.0)
            gs[0:ROWS] = (value[:ROWS] - positive).astype(jnp.bfloat16)
            gs[ROWS:count] = value[ROWS:].astype(jnp.bfloat16)
        else:
            gs[0:count] = value.astype(jnp.bfloat16)
        g = gs[0:count]
        iacc[rows] += dot(g, st[cols, :], NN)
        tacc[cols, :] += dot(g, si[rows], TN)

    def over(begin, end, one):
        lax.fori_loop(begin, end, lambda pair, _: (one(pair), 0)[1], 0)

    def relay(names):
        arrive(*[(name, part) for part in ("2a", "1b") for name in names])
        for name in names:
            hop(name, "2a", "4a", UP)
            hop(name, "1b", "4b", DOWN)

    def to_ring(names):
        for name in names:
            hop(name, "3", "6", UP)
            hop(name, "3", "5", DOWN)

    def near_across(name, chips):
        for chip in chips:
            arrive((name, {"3": "3", "1": "1a", "2": "2b"}[chip]))
            across(name, slot_of[chip])

    def far_to_side(names):
        arrive(*[(name, part) for part in ("4a", "4b") for name in names])
        for name in names:
            hop(name, "4", "7", SIDE)
        across(names[1], slot_of["4"])

    def late_across(name, chips):
        for chip in chips:
            arrive((name, chip))
            across(name, slot_of[chip])

    TEACHER, STUDENT = ("ti", "tt"), ("si", "st")
    relay(TEACHER)
    to_ring_first(STUDENT)
    near_across("tt", "312")
    far_to_side(TEACHER)
    arrive(*[("ti", part) for part in ("3", "1a", "2b")])
    arrive(*[("ttc", slot) for slot in range(4)])

    def teach_first(pair):
        pa1[pair] = teach(0, 512, pair)

    over(0, 2, teach_first)
    near_across("st", "3")
    relay(STUDENT)
    arrive(("si", "3"))
    to_ring(TEACHER)
    to_ring(STUDENT)
    arrive(("stc", 0), ("stc", 1))
    learn(0, 256, 0, pa1[0, 0:256], True)
    near_across("st", "12")
    arrive(("si", "1a"), ("si", "2b"))
    learn(256, 256, 0, pa1[0, 256:512])
    far_to_side(STUDENT)
    arrive(("stc", 2), ("stc", 3))
    learn(0, 512, 1, pa1[1])

    late_across("tt", "7")
    arrive(("ti", "7"))

    def teach_new2(pair):
        pn2[pair] = teach(512, 256, pair)

    over(0, 2, teach_new2)
    arrive(("ttc", 4), ("ttc", 5))
    pa2[...] = teach(0, 768, 2)

    late_across("st", "7")
    arrive(("si", "7"))
    over(0, 2, lambda pair: learn(512, 256, pair, pn2[pair]))
    arrive(("stc", 4), ("stc", 5))
    learn(0, 768, 2, pa2[...])

    late_across("tt", "56")
    arrive(("ti", "5"), ("ti", "6"))

    def teach_new3(pair):
        pn3[pair] = teach(768, 256, pair)

    over(0, 3, teach_new3)
    arrive(("ttc", 6), ("ttc", 7))
    pa3[...] = teach(0, 1024, 3)

    late_across("st", "56")
    arrive(("si", "5"), ("si", "6"))
    def give(slots):
        for p in slots:
            lo = p * 2 * ROWS + ROWS
            tb[p * ROWS : (p + 1) * ROWS] = tacc[lo : lo + ROWS].astype(jnp.bfloat16)
        for p in slots:
            rows = pl.ds(p * ROWS, ROWS)
            got["g", p] = remote(tb.at[rows], crecv.at[rows], csend_g.at[p], crecv_g.at[p], twin)

    def img_part(chip):
        slot = slot_of[chip]
        return iacc[slot * ROWS : (slot + 1) * ROWS]

    def txt_part(chip):
        slot = slot_of[chip]
        mine = tacc[slot * 2 * ROWS : slot * 2 * ROWS + ROWS]
        return mine + crecv[slot * ROWS : (slot + 1) * ROWS].astype(jnp.float32)

    part = {"i": img_part, "t": txt_part}
    out_buf = {"i": ib, "t": ts}
    in_buf = {"i": irecv, "t": trecv}
    out_sem = {"i": isend, "t": tsend}
    in_sem = {"i": irsem, "t": trsem}
    peers = {"i": img_devs, "t": txt_devs}
    piece = {"1": (0, ROWS, 0), "2": (ROWS, ROWS, 1), "3": (2 * ROWS, ROWS, 2), "4": (3 * ROWS, ROWS, 3),
             "5": (4 * ROWS, ROWS, 4), "6": (5 * ROWS, ROWS, 5), "7": (6 * ROWS, ROWS, 6)}
    QUARTER = ROWS // 4
    piece["1a"] = (0, HALF, 0)
    piece["2b"] = (ROWS + HALF, HALF, 1)
    for i, (chip, half) in enumerate((("1", "b"), ("2", "a"), ("4", "a"), ("4", "b"))):
        row = piece[chip][0] + (HALF if half == "b" else 0)
        for q in (0, 1):
            piece[chip + half + str(q)] = (row + q * QUARTER, QUARTER, 7 + 2 * i + q)

    for chip, sems in (("3", (2, 3)), ("5", (4, 15)), ("6", (5, 16))):
        row = piece[chip][0]
        piece[chip + "a"] = (row, HALF, sems[0])
        piece[chip + "b"] = (row + HALF, HALF, sems[1])

    def rows_of(ref, key):
        row, count, _ = piece[key]
        return ref[row : row + count]

    def fill(stream, key, value):
        row, count, _ = piece[key]
        out_buf[stream][row : row + count] = value.astype(jnp.bfloat16)

    def put(stream, key, way):
        row, count, sem = piece[key]
        rows = pl.ds(row, count)
        got[stream, "sum" + key] = remote(
            out_buf[stream].at[rows], in_buf[stream].at[rows],
            out_sem[stream].at[sem], in_sem[stream].at[sem], peers[stream][way],
        )

    def came(stream, key):
        arrive((stream, "sum" + key))
        return rows_of(in_buf[stream], key).astype(jnp.float32)

    def send_7(stream):
        fill(stream, "7", part[stream]("7"))
        put(stream, "7", SIDE)

    def send_near(stream):
        fill(stream, "1", part[stream]("1"))
        fill(stream, "2", part[stream]("2"))
        put(stream, "1a", UP)
        put(stream, "2b", DOWN)

    def send_56(stream):
        fill(stream, "5", part[stream]("5"))
        fill(stream, "6", part[stream]("6"))
        for half in "ab":
            put(stream, "5" + half, UP)
            put(stream, "6" + half, DOWN)

    def send_far(stream):
        fill(stream, "4", part[stream]("4") + came(stream, "7"))
        for q in "01":
            put(stream, "4b" + q, UP)
            put(stream, "4a" + q, DOWN)

    def send_side(stream, half):
        low = 0 if half == "a" else HALF
        own = part[stream]("3")[low : low + HALF]
        fill(stream, "3" + half, own + came(stream, "5" + half) + came(stream, "6" + half))
        put(stream, "3" + half, SIDE)

    def send_rest(stream, q):
        low, high = q * QUARTER, (q + 1) * QUARTER
        one, two, q = part[stream]("1"), part[stream]("2"), str(q)
        fill(stream, "1b" + q, one[HALF + low : HALF + high] + came(stream, "4b" + q))
        put(stream, "1b" + q, UP)
        fill(stream, "2a" + q, two[low:high] + came(stream, "4a" + q))
        put(stream, "2a" + q, DOWN)

    def total(stream):
        for key in ("1a", "1b0", "1b1", "2a0", "2a1", "2b", "3a", "3b"):
            arrive((stream, "sum" + key))
        near = rows_of(in_buf[stream], "1").astype(jnp.float32) + rows_of(in_buf[stream], "2").astype(jnp.float32)
        return logit_scale * (part[stream]("0") + near + rows_of(in_buf[stream], "3").astype(jnp.float32))

    learn(768, 256, 1, pn3[1])
    give((2, 3))
    learn(768, 256, 2, pn3[2])
    give((5, 4))
    arrive(("stc", 6), ("stc", 7))
    learn(256, 256, 3, pa3[256:512])
    send_near("i")
    arrive(("g", 2), ("g", 3))
    send_near("t")
    learn(512, 256, 3, pa3[512:768])
    send_7("i")
    arrive(("g", 5))
    send_7("t")
    learn(0, 256, 3, pa3[0:256])
    learn(768, 256, 3, pa3[768:1024])
    give((6, 7))
    learn(768, 256, 0, pn3[0])
    give((1, 0))
    send_56("i")
    arrive(("g", 6), ("g", 7))
    send_56("t")
    arrive(("g", 4))
    send_far("i")
    send_far("t")
    arrive(("g", 1))
    for half in "ab":
        send_side("i", half)
        send_side("t", half)
    for q in (0, 1):
        send_rest("i", q)
        send_rest("t", q)
    grads[0:ROWS] = back(total("i"), img_raw[...])
    arrive(("g", 0))
    grads[ROWS : 2 * ROWS] = back(total("t"), txt_raw[...])

    for copy in sent:
        copy.wait_send()


def body(student_img, student_txt, teacher_img, teacher_txt):
    width = student_img.shape[1]
    t_width = teacher_img.shape[1]
    bf16, f32 = jnp.bfloat16, jnp.float32
    vmem = pl.BlockSpec(memory_space=pltpu.VMEM)
    dma = pltpu.SemaphoreType.DMA((17,))
    both = pl.pallas_call(
        kernel,
        out_shape=jax.ShapeDtypeStruct((2 * ROWS, width), f32),
        in_specs=[pl.BlockSpec(memory_space=pl.ANY)] * 4,
        out_specs=vmem,
        scratch_shapes=[
            pltpu.VMEM((ROWS, width), bf16),
            pltpu.VMEM((ROWS, width), bf16),
            pltpu.VMEM((ROWS, t_width), bf16),
            pltpu.VMEM((ROWS, t_width), bf16),
            pltpu.VMEM((8 * ROWS, width), bf16),
            pltpu.VMEM((8 * ROWS, t_width), bf16),
            pltpu.VMEM((16 * ROWS, width), bf16),
            pltpu.VMEM((16 * ROWS, t_width), bf16),
            pltpu.VMEM((2, 4 * ROWS, 4 * ROWS), f32),
            pltpu.VMEM((2, 2 * ROWS, 4 * ROWS), f32),
            pltpu.VMEM((6 * ROWS, 4 * ROWS), f32),
            pltpu.VMEM((3, 2 * ROWS, 4 * ROWS), f32),
            pltpu.VMEM((8 * ROWS, 4 * ROWS), f32),
            pltpu.VMEM((8 * ROWS, 4 * ROWS), bf16),
            pltpu.VMEM((8 * ROWS, width), f32),
            pltpu.VMEM((16 * ROWS, width), f32),
            pltpu.VMEM((8 * ROWS, width), bf16),
            pltpu.VMEM((8 * ROWS, width), bf16),
            pltpu.VMEM((8 * ROWS, width), bf16),
            pltpu.VMEM((8 * ROWS, width), bf16),
            pltpu.VMEM((7 * ROWS, width), bf16),
            pltpu.VMEM((7 * ROWS, width), bf16),
        ]
        + [dma] * 19,
        compiler_params=pltpu.CompilerParams(
            collective_id=0, has_side_effects=True, vmem_limit_bytes=62 << 20
        ),
    )(student_img, student_txt, teacher_img, teacher_txt)
    return both[:ROWS], both[ROWS:]


def solution(mesh):
    rows = P(("blk", "narrow"), None)
    return jax.shard_map(body, mesh=mesh, in_specs=(rows,) * 4, out_specs=(rows, rows), check_vma=False)
```

```python
import jax
import jax.numpy as jnp
from jax import lax
from jax.experimental import pallas as pl
from jax.experimental.pallas import tpu as pltpu
from jax.sharding import PartitionSpec as P

epsilon = 1e-06
logit_scale = 100.0
logit_bias = -4.0
half_scale = 0.5 * logit_scale
half_bias = 0.5 * logit_bias

ROWS = 128
MESH_ID = pl.DeviceIdType.MESH
NT = (((1,), (1,)), ((), ()))
NN = (((1,), (0,)), ((), ()))
TN = (((0,), (0,)), ((), ()))

HALF = ROWS // 2


def dot(a, b, dims):
    return lax.dot_general(a, b, dims, preferred_element_type=jnp.float32)


def unit_of(raw):
    x = raw.astype(jnp.float32)
    radius = jnp.sqrt(jnp.sum(x * x, axis=1, keepdims=True) + epsilon)
    return x / radius, radius


def back(grad, raw):
    unit, radius = unit_of(raw)
    along = jnp.sum(unit * grad, axis=1, keepdims=True)
    return (grad - unit * along) / radius


def kernel(
    img_hbm, txt_hbm, timg_hbm, ttxt_hbm, grads, img_raw, txt_raw, timg_raw, ttxt_raw,
    si, ti, st, tt, pa1, pn2, pa2, pn3, pa3, gs, iacc, tacc, ib, tb, ts, crecv, irecv, trecv,
    send_si, send_ti, send_st, send_tt, recv_si, recv_ti, recv_st, recv_tt,
    csend_st, csend_tt, crecv_st, crecv_tt, csend_g, crecv_g, load, isend, irsem, tsend, trsem,
):
    b = lax.axis_index("blk")
    n = lax.axis_index("narrow")
    core = lax.rem(b, 2)
    z = b // 4
    x = 2 * lax.rem(b // 2, 2) + n // 4
    y = lax.rem(n, 4)
    odd = lax.rem(x, 2)

    def device(x, y, z, core):
        return ((z * 2 + x // 2) * 2 + core, lax.rem(x, 2) * 4 + y)

    def step(v, by):
        return lax.rem(v + 4 + by, 4)

    x_img = x + 1 - 2 * odd
    x_txt = lax.rem(x + 3 + 2 * odd, 4)
    img_up = device(x, step(y, 1), z, core)
    img_down = device(x, step(y, -1), z, core)
    img_side = device(x_img, y, z, core)
    txt_up = device(x, y, step(z, 1), core)
    txt_down = device(x, y, step(z, -1), core)
    txt_side = device(x_txt, y, z, core)
    twin = device(x, y, z, 1 - core)

    barrier = pltpu.get_barrier_semaphore()
    for peer in (img_up, img_down, img_side, txt_up, txt_down, txt_side, twin):
        pl.semaphore_signal(barrier, inc=1, device_id=peer, device_id_type=MESH_ID)

    loads = [
        pltpu.make_async_copy(src, dst, load.at[i])
        for i, (src, dst) in enumerate(
            ((timg_hbm, timg_raw), (ttxt_hbm, ttxt_raw), (img_hbm, img_raw), (txt_hbm, txt_raw))
        )
    ]
    for copy in loads:
        copy.start()
    for copy in loads[:2]:
        copy.wait()
    ti[0:ROWS] = unit_of(timg_raw[...])[0].astype(jnp.bfloat16)
    tt[0:ROWS] = unit_of(ttxt_raw[...])[0].astype(jnp.bfloat16)

    pl.semaphore_wait(barrier, 7)

    sent = []

    def remote(src, dst, ssem, rsem, dev):
        copy = pltpu.make_async_remote_copy(
            src_ref=src, dst_ref=dst, send_sem=ssem, recv_sem=rsem, device_id=dev, device_id_type=MESH_ID
        )
        copy.start()
        sent.append(copy)
        return copy

    img_devs = (img_up, img_down, img_side)
    txt_devs = (txt_up, txt_down, txt_side)
    arrays = {
        "ti": (ti, send_ti, recv_ti, ROWS, img_devs),
        "si": (si, send_si, recv_si, ROWS, img_devs),
        "tt": (tt, send_tt, recv_tt, 2 * ROWS, txt_devs),
        "st": (st, send_st, recv_st, 2 * ROWS, txt_devs),
    }
    got = {}
    UP, DOWN, SIDE = 0, 1, 2
    slot_of = {"0": 0, "3": 1, "1": 2, "2": 3, "4": 4, "7": 5, "5": 6, "6": 7}
    places = {}
    for chip, slot in slot_of.items():
        places[chip] = (slot, 0, ROWS)
        places[chip + "a"] = (slot, 0, HALF)
        places[chip + "b"] = (slot, HALF, HALF)
    index = {k: i for i, k in enumerate(("1a", "1b", "2a", "2b", "3", "4a", "4b", "7", "5", "6"))}

    def hop(name, src, dst, way):
        ref, ssem, rsem, pitch, devs = arrays[name]
        s_slot, s_row, count = places[src]
        d_slot, d_row, _ = places[dst]
        got[name, dst] = remote(
            ref.at[pl.ds(s_slot * pitch + s_row, count)], ref.at[pl.ds(d_slot * pitch + d_row, count)],
            ssem.at[index[dst]], rsem.at[index[dst]], devs[way],
        )

    def across(name, slot):
        ref, _, _, pitch, _ = arrays[name]
        ssem, rsem = (csend_tt, crecv_tt) if name == "tt" else (csend_st, crecv_st)
        got[name + "c", slot] = remote(
            ref.at[pl.ds(slot * pitch, ROWS)], ref.at[pl.ds(slot * pitch + ROWS, ROWS)],
            ssem.at[slot], rsem.at[slot], twin,
        )

    def arrive(*keys):
        for key in keys:
            got[key].wait_recv()

    def to_ring_first(names):
        for name in names:
            hop(name, "0a", "2a", UP)
            hop(name, "0b", "1b", DOWN)
        for name in names:
            hop(name, "0b", "2b", UP)
            hop(name, "0a", "1a", DOWN)

    def to_side_first(names):
        for name in names:
            hop(name, "0", "3", SIDE)
        across(names[1], 0)

    to_ring_first(("ti", "tt"))
    to_side_first(("ti", "tt"))
    for copy in loads[2:]:
        copy.wait()
    si[0:ROWS] = unit_of(img_raw[...])[0].astype(jnp.bfloat16)
    st[0:ROWS] = unit_of(txt_raw[...])[0].astype(jnp.bfloat16)
    to_side_first(("si", "st"))

    def clear(i, _):
        rows = pl.ds(pl.multiple_of(i * ROWS, ROWS), ROWS)
        iacc[rows, :] = jnp.zeros((ROWS, iacc.shape[1]), jnp.float32)
        tacc[pl.ds(pl.multiple_of(i * 2 * ROWS, 2 * ROWS), 2 * ROWS), :] = jnp.zeros(
            (2 * ROWS, tacc.shape[1]), jnp.float32
        )
        return 0

    lax.fori_loop(0, 8, clear, 0)

    def teacher_value(zt):
        return 0.5 - 0.5 * jnp.tanh(half_scale * zt + half_bias)

    WIDE = 4 * ROWS

    def columns(pair):
        return pl.ds(pl.multiple_of(pair * WIDE, WIDE), WIDE)

    def teach(first, count, pair):
        return teacher_value(dot(ti[first : first + count], tt[columns(pair), :], NT))

    def learn(first, count, pair, teacher, diagonal=False):
        rows = slice(first, first + count)
        cols = columns(pair)
        value = jnp.tanh(half_scale * dot(si[rows], st[cols, :], NT) + half_bias) + teacher
        if diagonal:
            row = lax.broadcasted_iota(jnp.int32, (ROWS, WIDE), 0)
            col = lax.broadcasted_iota(jnp.int32, (ROWS, WIDE), 1)
            positive = jnp.where(row == col, 1.0, 0.0)
            gs[0:ROWS] = (value[:ROWS] - positive).astype(jnp.bfloat16)
            gs[ROWS:count] = value[ROWS:].astype(jnp.bfloat16)
        else:
            gs[0:count] = value.astype(jnp.bfloat16)
        g = gs[0:count]
        iacc[rows] += dot(g, st[cols, :], NN)
        tacc[cols, :] += dot(g, si[rows], TN)

    def over(begin, end, one):
        lax.fori_loop(begin, end, lambda pair, _: (one(pair), 0)[1], 0)

    def relay(names):
        arrive(*[(name, part) for part in ("2a", "1b") for name in names])
        for name in names:
            hop(name, "2a", "4a", UP)
            hop(name, "1b", "4b", DOWN)

    def to_ring(names):
        for name in names:
            hop(name, "3", "6", UP)
            hop(name, "3", "5", DOWN)

    def near_across(name, chips):
        for chip in chips:
            arrive((name, {"3": "3", "1": "1a", "2": "2b"}[chip]))
            across(name, slot_of[chip])

    def far_to_side(names):
        arrive(*[(name, part) for part in ("4a", "4b") for name in names])
        for name in names:
            hop(name, "4", "7", SIDE)
        across(names[1], slot_of["4"])

    def late_across(name, chips):
        for chip in chips:
            arrive((name, chip))
            across(name, slot_of[chip])

    TEACHER, STUDENT = ("ti", "tt"), ("si", "st")
    relay(TEACHER)
    to_ring_first(STUDENT)
    near_across("tt", "312")
    far_to_side(TEACHER)
    arrive(*[("ti", part) for part in ("3", "1a", "2b")])
    arrive(*[("ttc", slot) for slot in range(4)])

    def teach_first(pair):
        pa1[pair] = teach(0, 512, pair)

    over(0, 2, teach_first)
    near_across("st", "3")
    relay(STUDENT)
    arrive(("si", "3"))
    to_ring(TEACHER)
    to_ring(STUDENT)
    arrive(("stc", 0), ("stc", 1))
    learn(0, 256, 0, pa1[0, 0:256], True)
    near_across("st", "12")
    arrive(("si", "1a"), ("si", "2b"))
    learn(256, 256, 0, pa1[0, 256:512])
    far_to_side(STUDENT)
    arrive(("stc", 2), ("stc", 3))
    learn(0, 512, 1, pa1[1])

    late_across("tt", "7")
    arrive(("ti", "7"))

    def teach_new2(pair):
        pn2[pair] = teach(512, 256, pair)

    over(0, 2, teach_new2)
    arrive(("ttc", 4), ("ttc", 5))
    pa2[...] = teach(0, 768, 2)

    late_across("st", "7")
    arrive(("si", "7"))
    over(0, 2, lambda pair: learn(512, 256, pair, pn2[pair]))
    late_across("tt", "56")
    arrive(("stc", 4), ("stc", 5))
    learn(0, 768, 2, pa2[...])

    arrive(("ti", "5"), ("ti", "6"))

    def teach_new3(pair):
        pn3[pair] = teach(768, 256, pair)

    over(0, 3, teach_new3)
    arrive(("ttc", 6), ("ttc", 7))
    pa3[...] = teach(0, 1024, 3)

    late_across("st", "56")
    arrive(("si", "5"), ("si", "6"))
    def give(slots):
        for p in slots:
            lo = p * 2 * ROWS + ROWS
            tb[p * ROWS : (p + 1) * ROWS] = tacc[lo : lo + ROWS].astype(jnp.bfloat16)
        for p in slots:
            rows = pl.ds(p * ROWS, ROWS)
            got["g", p] = remote(tb.at[rows], crecv.at[rows], csend_g.at[p], crecv_g.at[p], twin)

    def img_part(chip):
        slot = slot_of[chip]
        return iacc[slot * ROWS : (slot + 1) * ROWS]

    def txt_part(chip):
        slot = slot_of[chip]
        mine = tacc[slot * 2 * ROWS : slot * 2 * ROWS + ROWS]
        return mine + crecv[slot * ROWS : (slot + 1) * ROWS].astype(jnp.float32)

    part = {"i": img_part, "t": txt_part}
    out_buf = {"i": ib, "t": ts}
    in_buf = {"i": irecv, "t": trecv}
    out_sem = {"i": isend, "t": tsend}
    in_sem = {"i": irsem, "t": trsem}
    peers = {"i": img_devs, "t": txt_devs}
    piece = {"1": (0, ROWS, 0), "2": (ROWS, ROWS, 1), "3": (2 * ROWS, ROWS, 2), "4": (3 * ROWS, ROWS, 3),
             "5": (4 * ROWS, ROWS, 4), "6": (5 * ROWS, ROWS, 5), "7": (6 * ROWS, ROWS, 6)}
    QUARTER = ROWS // 4
    piece["1a"] = (0, HALF, 0)
    piece["2b"] = (ROWS + HALF, HALF, 1)
    for i, (chip, half) in enumerate((("1", "b"), ("2", "a"), ("4", "a"), ("4", "b"))):
        row = piece[chip][0] + (HALF if half == "b" else 0)
        for q in (0, 1):
            piece[chip + half + str(q)] = (row + q * QUARTER, QUARTER, 7 + 2 * i + q)

    for chip, sems in (("3", (2, 3)), ("5", (4, 15)), ("6", (5, 16))):
        row = piece[chip][0]
        piece[chip + "a"] = (row, HALF, sems[0])
        piece[chip + "b"] = (row + HALF, HALF, sems[1])

    def rows_of(ref, key):
        row, count, _ = piece[key]
        return ref[row : row + count]

    def fill(stream, key, value):
        row, count, _ = piece[key]
        out_buf[stream][row : row + count] = value.astype(jnp.bfloat16)

    def put(stream, key, way):
        row, count, sem = piece[key]
        rows = pl.ds(row, count)
        got[stream, "sum" + key] = remote(
            out_buf[stream].at[rows], in_buf[stream].at[rows],
            out_sem[stream].at[sem], in_sem[stream].at[sem], peers[stream][way],
        )

    def came(stream, key):
        arrive((stream, "sum" + key))
        return rows_of(in_buf[stream], key).astype(jnp.float32)

    def send_7(stream):
        fill(stream, "7", part[stream]("7"))
        put(stream, "7", SIDE)

    def send_near(stream):
        fill(stream, "1", part[stream]("1"))
        fill(stream, "2", part[stream]("2"))
        put(stream, "1a", UP)
        put(stream, "2b", DOWN)

    def send_56(stream):
        fill(stream, "5", part[stream]("5"))
        fill(stream, "6", part[stream]("6"))
        for half in "ab":
            put(stream, "5" + half, UP)
            put(stream, "6" + half, DOWN)

    def send_far(stream):
        fill(stream, "4", part[stream]("4") + came(stream, "7"))
        for q in "01":
            put(stream, "4b" + q, UP)
            put(stream, "4a" + q, DOWN)

    def send_side(stream, half):
        low = 0 if half == "a" else HALF
        own = part[stream]("3")[low : low + HALF]
        fill(stream, "3" + half, own + came(stream, "5" + half) + came(stream, "6" + half))
        put(stream, "3" + half, SIDE)

    def send_rest(stream, q):
        low, high = q * QUARTER, (q + 1) * QUARTER
        one, two, q = part[stream]("1"), part[stream]("2"), str(q)
        fill(stream, "1b" + q, one[HALF + low : HALF + high] + came(stream, "4b" + q))
        put(stream, "1b" + q, UP)
        fill(stream, "2a" + q, two[low:high] + came(stream, "4a" + q))
        put(stream, "2a" + q, DOWN)

    def total(stream):
        for key in ("1a", "1b0", "1b1", "2a0", "2a1", "2b", "3a", "3b"):
            arrive((stream, "sum" + key))
        near = rows_of(in_buf[stream], "1").astype(jnp.float32) + rows_of(in_buf[stream], "2").astype(jnp.float32)
        return logit_scale * (part[stream]("0") + near + rows_of(in_buf[stream], "3").astype(jnp.float32))

    learn(768, 256, 1, pn3[1])
    give((2, 3))
    learn(768, 256, 2, pn3[2])
    give((5, 4))
    arrive(("stc", 6), ("stc", 7))
    learn(256, 256, 3, pa3[256:512])
    send_near("i")
    arrive(("g", 2), ("g", 3))
    send_near("t")
    learn(512, 256, 3, pa3[512:768])
    send_7("i")
    arrive(("g", 5))
    send_7("t")
    learn(0, 256, 3, pa3[0:256])
    learn(768, 256, 3, pa3[768:1024])
    give((6, 7))
    learn(768, 256, 0, pn3[0])
    send_56("i")
    arrive(("g", 6), ("g", 7))
    send_56("t")
    give((1, 0))
    arrive(("g", 4))
    send_far("i")
    send_far("t")
    arrive(("g", 1))
    for half in "ab":
        send_side("i", half)
        send_side("t", half)
    for q in (0, 1):
        send_rest("i", q)
        send_rest("t", q)
    grads[0:ROWS] = back(total("i"), img_raw[...])
    arrive(("g", 0))
    grads[ROWS : 2 * ROWS] = back(total("t"), txt_raw[...])

    for copy in sent:
        copy.wait_send()


def body(student_img, student_txt, teacher_img, teacher_txt):
    width = student_img.shape[1]
    t_width = teacher_img.shape[1]
    bf16, f32 = jnp.bfloat16, jnp.float32
    vmem = pl.BlockSpec(memory_space=pltpu.VMEM)
    dma = pltpu.SemaphoreType.DMA((17,))
    both = pl.pallas_call(
        kernel,
        out_shape=jax.ShapeDtypeStruct((2 * ROWS, width), f32),
        in_specs=[pl.BlockSpec(memory_space=pl.ANY)] * 4,
        out_specs=vmem,
        scratch_shapes=[
            pltpu.VMEM((ROWS, width), bf16),
            pltpu.VMEM((ROWS, width), bf16),
            pltpu.VMEM((ROWS, t_width), bf16),
            pltpu.VMEM((ROWS, t_width), bf16),
            pltpu.VMEM((8 * ROWS, width), bf16),
            pltpu.VMEM((8 * ROWS, t_width), bf16),
            pltpu.VMEM((16 * ROWS, width), bf16),
            pltpu.VMEM((16 * ROWS, t_width), bf16),
            pltpu.VMEM((2, 4 * ROWS, 4 * ROWS), f32),
            pltpu.VMEM((2, 2 * ROWS, 4 * ROWS), f32),
            pltpu.VMEM((6 * ROWS, 4 * ROWS), f32),
            pltpu.VMEM((3, 2 * ROWS, 4 * ROWS), f32),
            pltpu.VMEM((8 * ROWS, 4 * ROWS), f32),
            pltpu.VMEM((8 * ROWS, 4 * ROWS), bf16),
            pltpu.VMEM((8 * ROWS, width), f32),
            pltpu.VMEM((16 * ROWS, width), f32),
            pltpu.VMEM((8 * ROWS, width), bf16),
            pltpu.VMEM((8 * ROWS, width), bf16),
            pltpu.VMEM((8 * ROWS, width), bf16),
            pltpu.VMEM((8 * ROWS, width), bf16),
            pltpu.VMEM((7 * ROWS, width), bf16),
            pltpu.VMEM((7 * ROWS, width), bf16),
        ]
        + [dma] * 19,
        compiler_params=pltpu.CompilerParams(
            collective_id=0, has_side_effects=True, vmem_limit_bytes=62 << 20
        ),
    )(student_img, student_txt, teacher_img, teacher_txt)
    return both[:ROWS], both[ROWS:]


def solution(mesh):
    rows = P(("blk", "narrow"), None)
    return jax.shard_map(body, mesh=mesh, in_specs=(rows,) * 4, out_specs=(rows, rows), check_vma=False)
```
